32 devices in a mesh: ctx: 8 (over y, x, core), head: 4 (over z).
Axes of the slice: x: 2, y: 2, z: 4, core: 2. Of those that a mesh axis runs over, the one named last changes fastest.
Arguments:
- query_input: bfloat16 [1024, 2048], P(('ctx', 'head')), may hold values from -9 to 9
- key_input: bfloat16 [1024, 512], P(('ctx', 'head')), may hold values from -6 to 6
- value_input: bfloat16 [1024, 512], P(('ctx', 'head')), may hold values from -0.625 to 0.625
- output_gradient: bfloat16 [1024, 2048], P(('ctx', 'head')), may hold values from -6 to 6
- log_softmax_norm: float32 [1024, 32], P('ctx', 'head'), as said below
- output_delta_rows: float32 [1024, 32], P('ctx', 'head'), may hold values from -6 to 6
- positions: int32 [1024], P('ctx'), may hold values from 0 to 1023, as said below
Outputs:
- grad_query: bfloat16 [1024, 2048], P(('ctx', 'head'))
- key_gradient: bfloat16 [1024, 512], P(('ctx', 'head'))
- value_gradient: bfloat16 [1024, 512], P(('ctx', 'head'))
The draws below stay inside these ranges and needn't reach their ends.
Inputs may be any that keep to these rules, and one draw needn't show every extreme that they name: positions is a permutation of 0 to 1023; each aligned block of 128 rows holds 64 ascending consecutive positions starting at a 64, then 64 ascending consecutive positions starting at (15 - a) * 64, with a different number a in each block. log_softmax_norm of a row lies between log(p + 1) + 0.7 and log(p + 1) + 1.6, where p is the row's position.
All inputs are finite; a program needn't handle non-finite values.
Results may differ from the reference program's by a relative error of at most 0.0055.
Values may be sent and summed in bfloat16 or wider, within the bound.
No kernel may reach another device: no remote copies, remote signals or barrier semaphores. Data moves between devices by JAX's collectives and lax.ppermute only.
A program may use at most 64 MiB of HBM per device.

```python
import jax
import jax.numpy as jnp
from jax import lax

QUERY_HEADS = 32
KEY_VALUE_HEADS = 8
HEAD_WIDTH = 64
STRETCH = 128
SEQUENCE_TOKENS = 1024
N_CTX = 8


def paired_positions(key):
    block_count = SEQUENCE_TOKENS // STRETCH
    half_rows = STRETCH // 2
    leading = jax.random.permutation(jax.random.fold_in(key, 17), block_count).astype(jnp.int32)
    within = jnp.arange(half_rows, dtype=jnp.int32)
    front = leading[:, None] * half_rows + within[None, :]
    back = (2 * block_count - 1 - leading)[:, None] * half_rows + within[None, :]
    return jnp.concatenate([front, back], axis=1).reshape(SEQUENCE_TOKENS).astype(jnp.int32)


def draw_positions(key, part):
    return paired_positions(key)


def draw_log_softmax_norm(key, part):
    base = jnp.log(paired_positions(key).astype(jnp.float32) + 1.0)[:, None]
    sample = jax.random.uniform(jax.random.fold_in(key, 29), (SEQUENCE_TOKENS, QUERY_HEADS), jnp.float32)
    offset_rows = 0.8 + 0.7 * sample
    return (base + offset_rows).astype(jnp.float32)


def levels(stream_key, extent, shards, least, high):
    level = 1.0
    for axis_at, parts in shards:
        draws = jax.random.uniform(jax.random.fold_in(jax.random.fold_in(stream_key, 6), axis_at), (parts,), jnp.float32, least / len(shards), high / len(shards))
        level = level * jnp.repeat(jnp.exp(draws), extent[axis_at] // parts).reshape((-1,) + (1,) * (len(extent) - 1 - axis_at))
    return level


def noise(key, extent, scale, limit, cuts=(), held_as=jnp.bfloat16):
    factor_of = levels(key, extent, cuts, -0.22, 0.18) if cuts else 1.0
    entries = jax.random.normal(key, extent, jnp.float32) * scale * factor_of
    return jnp.minimum(jnp.maximum(entries, -limit), limit).astype(held_as)


def setup_inputs(seed: int = 0) -> dict:
    seeds = jax.random.split(jax.random.key(seed), 8)
    return {
        "query_input": noise(seeds[0], (SEQUENCE_TOKENS, QUERY_HEADS * HEAD_WIDTH), 1.5, 9.0, ((0, 32),)),
        "key_input": noise(seeds[1], (SEQUENCE_TOKENS, KEY_VALUE_HEADS * HEAD_WIDTH), 1.0, 6.0, ((0, 32),)),
        "value_input": noise(seeds[2], (SEQUENCE_TOKENS, KEY_VALUE_HEADS * HEAD_WIDTH), 0.1, 0.625, ((0, 32),)),
        "output_gradient": noise(seeds[3], (SEQUENCE_TOKENS, QUERY_HEADS * HEAD_WIDTH), 1.0, 6.0, ((0, 32),)),
        "log_softmax_norm": draw_log_softmax_norm(jax.random.fold_in(seeds[7], 71), 0),
        "output_delta_rows": noise(seeds[5], (SEQUENCE_TOKENS, QUERY_HEADS), 1.0, 6.0, ((0, 8), (1, 4)), jnp.float32),
        "positions": draw_positions(jax.random.fold_in(seeds[7], 71), 0),
    }


def to_bfloat_exact(values_f32):
    return lax.optimization_barrier(values_f32.astype(jnp.bfloat16)).astype(jnp.float32)


def head_backward(operands, positions_f32, score_scale, block_rows):
    query_head, key_head, value_head, grad_head, norm_head, delta_head = operands
    sequence_length = query_head.shape[0]
    block_total = sequence_length // block_rows

    def one_block(running, block_index):
        key_sum, value_sum = running
        first_row = block_index * block_rows
        query_block = lax.dynamic_slice_in_dim(query_head, first_row, block_rows, 0)
        grad_block = lax.dynamic_slice_in_dim(grad_head, first_row, block_rows, 0)
        norm_block = lax.dynamic_slice_in_dim(norm_head, first_row, block_rows, 0)
        delta_block = lax.dynamic_slice_in_dim(delta_head, first_row, block_rows, 0)
        pos_block = lax.dynamic_slice_in_dim(positions_f32, first_row, block_rows, 0)
        scores = jnp.einsum("qgd,kd->qgk", query_block, key_head) * score_scale
        visible = (pos_block[:, None] >= positions_f32[None, :])[:, None, :]
        probabilities = jnp.where(visible, jnp.exp(scores - norm_block[:, :, None]), 0.0)
        grad_prob = jnp.einsum("qgd,kd->qgk", grad_block, value_head)
        grad_score = probabilities * (grad_prob - delta_block[:, :, None])
        prob_rounded = to_bfloat_exact(probabilities)
        score_rounded = to_bfloat_exact(grad_score)
        value_sum = value_sum + jnp.einsum("qgk,qgd->kd", prob_rounded, grad_block)
        key_sum = key_sum + score_scale * jnp.einsum("qgk,qgd->kd", score_rounded, query_block)
        query_term = score_scale * jnp.einsum("qgk,kd->qgd", score_rounded, key_head)
        return (key_sum, value_sum), query_term

    zero_rows = jnp.zeros(key_head.shape, jnp.float32)
    (key_sum, value_sum), query_terms = lax.scan(one_block, (zero_rows, zero_rows), jnp.arange(block_total, dtype=jnp.int32))
    return query_terms.reshape(query_head.shape), key_sum, value_sum


def reference(query_input, key_input, value_input, output_gradient, log_softmax_norm, output_delta_rows, positions):
    query_group_width = QUERY_HEADS // KEY_VALUE_HEADS
    score_scale = HEAD_WIDTH ** -0.5
    sequence_length = query_input.shape[0]
    block_rows = STRETCH * 8 if N_CTX % 8 == 0 else STRETCH
    query_per_head = query_input.astype(jnp.float32).reshape(sequence_length, KEY_VALUE_HEADS, query_group_width, HEAD_WIDTH).transpose(1, 0, 2, 3)
    gradient_per_head = output_gradient.astype(jnp.float32).reshape(sequence_length, KEY_VALUE_HEADS, query_group_width, HEAD_WIDTH).transpose(1, 0, 2, 3)
    key_per_head = key_input.astype(jnp.float32).reshape(sequence_length, KEY_VALUE_HEADS, HEAD_WIDTH).transpose(1, 0, 2)
    value_per_head = value_input.astype(jnp.float32).reshape(sequence_length, KEY_VALUE_HEADS, HEAD_WIDTH).transpose(1, 0, 2)
    norm_per_head = log_softmax_norm.reshape(sequence_length, KEY_VALUE_HEADS, query_group_width).transpose(1, 0, 2)
    delta_per_head = output_delta_rows.reshape(sequence_length, KEY_VALUE_HEADS, query_group_width).transpose(1, 0, 2)
    positions_f32 = positions.astype(jnp.float32)

    def per_head(operands):
        return head_backward(operands, positions_f32, score_scale, block_rows)

    query_grads, key_gradient_heads, value_gradient_heads = lax.map(per_head, (query_per_head, key_per_head, value_per_head, gradient_per_head, norm_per_head, delta_per_head))
    grad_query = query_grads.transpose(1, 0, 2, 3).reshape(sequence_length, QUERY_HEADS * HEAD_WIDTH).astype(jnp.bfloat16)
    key_gradient = key_gradient_heads.transpose(1, 0, 2).reshape(sequence_length, KEY_VALUE_HEADS * HEAD_WIDTH).astype(jnp.bfloat16)
    value_gradient = value_gradient_heads.transpose(1, 0, 2).reshape(sequence_length, KEY_VALUE_HEADS * HEAD_WIDTH).astype(jnp.bfloat16)
    return grad_query, key_gradient, value_gradient
```

```python
import jax
import jax.numpy as jnp
from jax import lax
from jax.experimental import pallas as pl
from jax.experimental.pallas import tpu as pltpu
from jax.sharding import PartitionSpec as P

HEAD_WIDTH = 64
LANES = 128
PIECES = 2
MASKED = 16384.0
F32 = jnp.float32
BF16 = jnp.bfloat16


def for_sending(array):
    return jax.tree.map(lambda a: a.astype(jnp.bfloat16) if a.dtype == jnp.float32 else a, array)


def from_behind(array, axis, by):
    count = lax.axis_size(axis)
    return lax.ppermute(array, axis, [(i, (i + by) % count) for i in range(count)])


def block_terms(
    query, grad_rows, norm_rows, delta_part, query_pos, key_block, value_block, key_pos
):
    row_count = query.shape[0]
    col_count = key_block.shape[0]
    kv_heads = key_block.shape[1] // HEAD_WIDTH
    query_group_width = query.shape[1] // (kv_heads * HEAD_WIDTH)
    score_scale = HEAD_WIDTH ** (-0.5)
    query_per_head = query.reshape(row_count, kv_heads, query_group_width, HEAD_WIDTH)
    gradient_per_head = grad_rows.reshape(row_count, kv_heads, query_group_width, HEAD_WIDTH)
    key_per_head = key_block.reshape(col_count, kv_heads, HEAD_WIDTH)
    value_per_head = value_block.reshape(col_count, kv_heads, HEAD_WIDTH)
    scores = (
        jnp.einsum(
            "qhgd,khd->qhgk", query_per_head, key_per_head, preferred_element_type=jnp.float32
        )
        * score_scale
    )
    visible = (query_pos[:, None] >= key_pos[None, :])[:, None, None, :]
    norm_cols = norm_rows.reshape(row_count, kv_heads, query_group_width, 1)
    probabilities = jnp.where(visible, jnp.exp(scores - norm_cols), 0.0)
    grad_prob = jnp.einsum(
        "qhgd,khd->qhgk", gradient_per_head, value_per_head, preferred_element_type=jnp.float32
    )
    grad_score = probabilities * (
        grad_prob - delta_part.reshape(row_count, kv_heads, query_group_width, 1)
    )
    prob_rounded = probabilities.astype(jnp.bfloat16)
    score_rounded = grad_score.astype(jnp.bfloat16)
    value_term = jnp.einsum(
        "qhgk,qhgd->khd", prob_rounded, gradient_per_head, preferred_element_type=jnp.float32
    )
    key_term = score_scale * jnp.einsum(
        "qhgk,qhgd->khd", score_rounded, query_per_head, preferred_element_type=jnp.float32
    )
    query_term = score_scale * jnp.einsum(
        "qhgk,khd->qhgd", score_rounded, key_per_head, preferred_element_type=jnp.float32
    )
    return (
        query_term.reshape(row_count, -1),
        key_term.reshape(col_count, -1),
        value_term.reshape(col_count, -1),
    )


def no_terms(operands):
    query = operands[0]
    key_block = operands[5]
    return (
        jnp.zeros(query.shape, jnp.float32),
        jnp.zeros(key_block.shape, jnp.float32),
        jnp.zeros(key_block.shape, jnp.float32),
    )


def all_terms(operands):
    return block_terms(*operands)


def pair_terms(query, grad_rows, norm_rows, delta_part, query_pos, key_block, value_block, key_pos):
    row_half = query.shape[0] // 2
    col_half = key_block.shape[0] // 2
    zero_cols = jnp.zeros((col_half, key_block.shape[1]), jnp.float32)
    key_sums = [zero_cols, zero_cols]
    value_sums = [zero_cols, zero_cols]
    query_parts = []
    for row_side in range(2):
        rows_here = slice(row_side * row_half, (row_side + 1) * row_half)
        query_sum = jnp.zeros((row_half, query.shape[1]), jnp.float32)
        for col_side in range(2):
            cols_here = slice(col_side * col_half, (col_side + 1) * col_half)
            operands = (
                query[rows_here],
                grad_rows[rows_here],
                norm_rows[rows_here],
                delta_part[rows_here],
                query_pos[rows_here],
                key_block[cols_here],
                value_block[cols_here],
                key_pos[cols_here],
            )
            reached = jnp.any(query_pos[rows_here][:, None] >= key_pos[cols_here][None, :])
            query_term, key_term, value_term = lax.cond(reached, all_terms, no_terms, operands)
            query_sum = query_sum + query_term
            key_sums[col_side] = key_sums[col_side] + key_term
            value_sums[col_side] = value_sums[col_side] + value_term
        query_parts.append(query_sum)
    return (
        jnp.concatenate(query_parts, 0),
        jnp.concatenate(key_sums, 0),
        jnp.concatenate(value_sums, 0),
    )


def pass_keys(traveler, offset):
    return from_behind((for_sending(traveler[0]), for_sending(traveler[1])), "ctx", offset)


def pass_sums(traveler, offset):
    return from_behind((traveler[2], traveler[3], traveler[4]), "ctx", offset)


def on_device(
    query_input,
    key_input,
    value_input,
    output_gradient,
    log_softmax_norm,
    output_delta_rows,
    positions,
):
    query, key_local, value_local, grad_rows = (
        lax.all_to_all(query_input, "head", split_axis=1, concat_axis=0, tiled=True),
        lax.all_to_all(key_input, "head", split_axis=1, concat_axis=0, tiled=True),
        lax.all_to_all(value_input, "head", split_axis=1, concat_axis=0, tiled=True),
        lax.all_to_all(output_gradient, "head", split_axis=1, concat_axis=0, tiled=True),
    )
    query_pos = positions.astype(jnp.float32)
    row_count = query.shape[0]
    feature_width = key_local.shape[1]
    grad_query = jnp.zeros(query.shape, jnp.float32)

    def visit(key_block, value_block, key_pos):
        return pair_terms(
            query,
            grad_rows,
            log_softmax_norm,
            output_delta_rows,
            query_pos,
            key_block,
            value_block,
            key_pos,
        )

    offsets = (1,)
    bounds = ((0, row_count),)
    travelers = tuple(
        (
            (
                key_local,
                value_local,
                jnp.zeros((upper_row - lower_row, feature_width), jnp.float32),
                jnp.zeros((upper_row - lower_row, feature_width), jnp.float32),
                query_pos,
            )
            for lower_row, upper_row in bounds
        )
    )

    def absorb_all(query_sum, travelers):
        updated = []
        for traveler in travelers:
            key_block, value_block, key_acc, value_acc, key_pos = traveler
            query_term, key_term, value_term = visit(key_block, value_block, key_pos)
            query_sum = query_sum + query_term
            updated.append(
                (key_block, value_block, key_acc + key_term, value_acc + value_term, key_pos)
            )
        return (query_sum, tuple(updated))

    def cycle_turn(turn_index, running):
        query_sum, travelers = absorb_all(running[0], running[1])
        moved = []
        for traveler, offset in zip(travelers, offsets):
            key_block, value_block = pass_keys(traveler, offset)
            key_acc, value_acc, key_pos = pass_sums(traveler, offset)
            moved.append((key_block, value_block, key_acc, value_acc, key_pos))
        return (query_sum, tuple(moved))

    grad_query, travelers = lax.fori_loop(
        0, lax.axis_size("ctx") - 1, cycle_turn, (grad_query, travelers)
    )
    grad_query, travelers = absorb_all(grad_query, travelers)
    returned = [pass_sums(traveler, offset) for traveler, offset in zip(travelers, offsets)]
    key_gradient = jnp.concatenate([arrived[0] for arrived in returned], 0)
    value_gradient = jnp.concatenate([arrived[1] for arrived in returned], 0)
    query_out, key_out, value_out = (
        lax.all_to_all(
            grad_query.astype(jnp.bfloat16), "head", split_axis=0, concat_axis=1, tiled=True
        ),
        lax.all_to_all(
            key_gradient.astype(jnp.bfloat16), "head", split_axis=0, concat_axis=1, tiled=True
        ),
        lax.all_to_all(
            value_gradient.astype(jnp.bfloat16), "head", split_axis=0, concat_axis=1, tiled=True
        ),
    )
    return (query_out, key_out, value_out)


def lane_of(shape):
    return lax.broadcasted_iota(jnp.int32, shape, len(shape) - 1)


def pack_kernel(pos_ref, q_ref, g_ref, k_ref, v_ref, n_ref, d_ref, out_ref, wide_ref):
    rows = q_ref.shape[0]
    planes = n_ref.shape[0] // rows
    block = lax.axis_index("ctx")
    kv_heads = out_ref.shape[0]
    group = q_ref.shape[1] // k_ref.shape[1]
    lane = lane_of((rows, LANES))
    low = lane < HEAD_WIDTH
    scale = HEAD_WIDTH ** (-0.5)
    for m in range(q_ref.shape[1] // LANES):
        cols = slice(m * LANES, (m + 1) * LANES)
        q = q_ref[:, cols].astype(F32) * scale
        g = g_ref[:, cols].astype(F32)
        c, e = (2 * m) // group, (2 * m) % group
        even = jnp.where(low, q, pltpu.roll(g, HEAD_WIDTH, 1))
        odd = jnp.where(low, pltpu.roll(q, HEAD_WIDTH, 1), g)
        out_ref[c, e * rows : (e + 1) * rows, :] = even.astype(BF16)
        out_ref[c, (e + 1) * rows : (e + 2) * rows, :] = odd.astype(BF16)
    at = group * rows
    for m in range(k_ref.shape[1] // LANES):
        cols = slice(m * LANES, (m + 1) * LANES)
        k = k_ref[:, cols].astype(F32)
        v = v_ref[:, cols].astype(F32)
        even = jnp.where(low, k, pltpu.roll(v, HEAD_WIDTH, 1))
        odd = jnp.where(low, pltpu.roll(k, HEAD_WIDTH, 1), v)
        out_ref[2 * m, at : at + rows, :] = even.astype(BF16)
        out_ref[2 * m + 1, at : at + rows, :] = odd.astype(BF16)
    at = at + rows
    tall = n_ref.shape[0]
    wide_ref[...] = jnp.zeros(wide_ref.shape, F32)
    wide_ref[0, :, 0 : n_ref.shape[1]] = n_ref[...]
    wide_ref[1, :, 0 : d_ref.shape[1]] = d_ref[...]
    tall_lane = lane_of((tall, LANES))
    row_half = tall // 2
    lead = (pos_ref[0] // row_half).astype(F32)
    for parity in range(2):
        spread = jnp.zeros((tall, LANES), F32)
        for t in range(2):
            rest = wide_ref[t]
            for s in range(PIECES):
                piece = rest.astype(BF16).astype(F32)
                rest = rest - piece
                to = s * 2 * group + t * group
                here = (tall_lane >= to) & (tall_lane < to + group)
                moved = pltpu.roll(piece, (to - group * parity) % LANES, 1)
                spread = jnp.where(here, moved, spread)
        width = PIECES * 2 * group
        tile = jnp.zeros((rows, LANES), F32)
        for h in range(planes):
            part = spread[h * rows : (h + 1) * rows]
            moved = pltpu.roll(part, h * width, 1) if h else part
            tile = jnp.where((lane >= h * width) & (lane < (h + 1) * width), moved, tile)
        first = planes * width
        mine = (lane >= first) & (lane < first + planes * kv_heads) & (lane % kv_heads == block)
        tile = jnp.where(mine, lead, tile).astype(BF16)
        for c in range(parity, kv_heads, 2):
            out_ref[c, at : at + rows, :] = tile


def spread_kernel(in_ref, own_ref, *send_refs):
    blocks, double, _ = in_ref.shape
    rows = double // 2
    plane = lax.axis_index("head")
    width = LANES // blocks
    lane = lane_of((rows, LANES))
    kv = in_ref[:, 0:rows, :].reshape(blocks * rows, LANES)
    tiles = [in_ref[b, rows:double, :].astype(F32) for b in range(blocks)]
    for j in range(len(send_refs) + 1):
        wanted = plane ^ j
        tile = jnp.zeros((rows, LANES), F32)
        for b in range(blocks):
            shift = lax.rem(b * width - wanted * width + LANES, LANES)
            here = (lane >= b * width) & (lane < (b + 1) * width)
            tile = jnp.where(here, pltpu.roll(tiles[b], shift, 1), tile)
        if j == 0:
            own_ref[...] = tile.astype(BF16)
        else:
            send_refs[j - 1][0 : blocks * rows, :] = kv
            send_refs[j - 1][blocks * rows : (blocks + 1) * rows, :] = tile.astype(BF16)


def make_attend(planes):
    def attend_kernel(in_ref, own_ref, *refs):
        got = refs[: planes - 1]
        out_ref, sum_ref = refs[planes - 1 : planes + 1]
        send_refs = refs[planes + 1 : 2 * planes]
        left_ref, right_ref, both_ref, prob_ref, score_ref = refs[2 * planes :]
        blocks = in_ref.shape[0]
        rows = own_ref.shape[0]
        group = in_ref.shape[1] // rows - 2
        tokens = blocks * rows
        width = LANES // blocks
        plane = lax.axis_index("head")
        holder = plane ^ (lax.axis_index("ctx") // (blocks // planes))
        lane = lane_of((rows, LANES))
        lane_row = lane_of((1, LANES))
        first = planes * width

        tile = own_ref[...].astype(F32)
        for j in range(1, planes):
            other = got[j - 1][tokens : tokens + rows, :].astype(F32)
            tile = jnp.where(holder == j, other, tile)
        folds = (tile, pltpu.roll(tile, LANES // 2, 1))

        lead = jnp.zeros((1, LANES), F32)
        for b in range(blocks):
            at = (group + 1) * rows
            lead = lead + in_ref[b, at : at + rows, :].astype(F32)[0:1]
        key_plane = (lane_row - first) // blocks
        per_half = planes // 2
        count = 2 * blocks

        def place(lead_of, which):
            front = per_half * lead_of + which
            back = per_half * (count - 1 - lead_of) + (which - per_half)
            return jnp.where(which < per_half, front, back)

        key_place = place(lead, key_plane.astype(F32))
        in_mask = (lane_row >= first) & (lane_row < first + planes * blocks)

        low = lane_of((tokens, LANES)) < HEAD_WIDTH
        nothing = jnp.zeros((tokens, LANES), BF16)
        for e in range(group):
            pair = in_ref[:, e * rows : (e + 1) * rows, :].reshape(tokens, LANES)
            both_ref[e * tokens : (e + 1) * tokens, :] = pair
            right_ref[e, 0:tokens, 0:LANES] = jnp.where(low, pair, nothing)
            right_ref[e, tokens : 2 * tokens, 0:LANES] = jnp.where(low, nothing, pair)
        for b in range(blocks):
            lead_b = jnp.sum(
                jnp.where(lane_row == first + b, lead, 0.0), axis=1, keepdims=True
            )
            query_place = place(lead_b, plane.astype(F32))
            hidden = jnp.where(in_mask & (key_place > query_place), MASKED, 0.0)
            fold = folds[(b * width) // (LANES // 2)]
            at = (b * width) % (LANES // 2)
            near = (lane >= at) & (lane < at + width)
            for e in range(group):
                norm = jnp.where(near & (lane % (2 * group) == e), fold, hidden)
                delta = jnp.where(near & (lane % (2 * group) == group + e), fold, 0.0)
                down = slice(b * rows, (b + 1) * rows)
                right_ref[e, down, LANES:] = norm.astype(BF16)
                down = slice(tokens + b * rows, tokens + (b + 1) * rows)
                right_ref[e, down, LANES:] = delta.astype(BF16)

        key_row = lax.broadcasted_iota(jnp.int32, (tokens, LANES), 0)
        wide_lane = lane_of((tokens, LANES))
        square_key = lax.broadcasted_iota(jnp.int32, (tokens, tokens), 0)
        square_query = lane_of((tokens, tokens))
        allowed = (square_key <= square_query) | (square_key // rows != square_query // rows)
        query_sum = None
        for j in range(planes):
            if j == 0:
                kv = in_ref[:, group * rows : (group + 1) * rows, :].reshape(tokens, LANES)
            else:
                kv = got[j - 1][0:tokens, :]
            mark = first + (plane ^ j) * blocks + key_row // rows
            ones = jnp.where((wide_lane < first) | (wide_lane == mark), -1.0, 0.0)
            left_ref[:, 0:LANES] = kv
            left_ref[:, LANES:] = ones.astype(BF16)
            for e in range(group):
                both = lax.dot_general(
                    left_ref[...],
                    right_ref[e],
                    (((1,), (1,)), ((), ())),
                    preferred_element_type=F32,
                )
                prob = jnp.exp(both[:, 0:tokens])
                if j == 0:
                    prob = jnp.where(allowed, prob, 0.0)
                score = prob * both[:, tokens:]
                across = slice(e * tokens, (e + 1) * tokens)
                prob_ref[:, across] = prob.astype(BF16)
                score_ref[:, across] = score.astype(BF16)
            value_side = jnp.dot(prob_ref[...], both_ref[...], preferred_element_type=F32)
            key_side = jnp.dot(score_ref[...], both_ref[...], preferred_element_type=F32)
            kv_sum = jnp.where(low, key_side, value_side)
            if j == 0:
                sum_ref[...] = kv_sum
            else:
                send_refs[j - 1][...] = kv_sum.astype(BF16)
            turned = kv.astype(F32).T[0:HEAD_WIDTH].astype(BF16)
            part = jnp.dot(turned, score_ref[...], preferred_element_type=F32)
            query_sum = part if query_sum is None else query_sum + part
        scale = HEAD_WIDTH ** (-0.5)
        for m in range(group // 2):
            pair = jnp.concatenate(
                [
                    query_sum[:, 2 * m * tokens : (2 * m + 1) * tokens],
                    query_sum[:, (2 * m + 1) * tokens : (2 * m + 2) * tokens],
                ],
                0,
            )
            done = (pair.T * scale).astype(BF16)
            out_ref[:, m * rows : (m + 1) * rows, :] = done.reshape(blocks, rows, LANES)

    return attend_kernel


def total_kernel(sum_ref, *refs):
    got, out_ref = refs[:-2], refs[-1]
    total = sum_ref[...]
    for ref in got:
        total = total + ref[...].astype(F32)
    out_ref[...] = total.astype(BF16).reshape(out_ref.shape)


def unpack_kernel(in_ref, q_ref, k_ref, v_ref):
    rows = q_ref.shape[0]
    heads = in_ref.shape[0]
    tiles = in_ref.shape[1] // rows - 1
    low = lane_of((rows, LANES)) < HEAD_WIDTH
    for c in range(heads):
        for m in range(tiles):
            at = (c * tiles + m) * LANES
            q_ref[:, at : at + LANES] = in_ref[c, m * rows : (m + 1) * rows, :]
    for m in range(heads // 2):
        even = in_ref[2 * m, tiles * rows : (tiles + 1) * rows, :].astype(F32)
        odd = in_ref[2 * m + 1, tiles * rows : (tiles + 1) * rows, :].astype(F32)
        cols = slice(m * LANES, (m + 1) * LANES)
        k_ref[:, cols] = jnp.where(low, even, pltpu.roll(odd, HEAD_WIDTH, 1)).astype(BF16)
        v_ref[:, cols] = jnp.where(low, pltpu.roll(even, HEAD_WIDTH, 1), odd).astype(BF16)


def whole(shape):
    return pl.BlockSpec(shape, lambda: (0,) * len(shape))


def by_heads(
    query_input,
    key_input,
    value_input,
    output_gradient,
    log_softmax_norm,
    output_delta_rows,
    positions,
):
    blocks = lax.axis_size("ctx")
    planes = lax.axis_size("head")
    rows = query_input.shape[0]
    tokens = blocks * rows
    group = query_input.shape[1] // key_input.shape[1]
    packet = (group + 2) * rows
    tall = positions.shape[0]
    packed = pl.pallas_call(
        pack_kernel,
        name="pack",
        out_shape=jax.ShapeDtypeStruct((blocks, packet, LANES), BF16),
        in_specs=[pl.BlockSpec(memory_space=pltpu.SMEM)]
        + [
            whole(a.shape)
            for a in (
                query_input,
                output_gradient,
                key_input,
                value_input,
                log_softmax_norm,
                output_delta_rows,
            )
        ],
        out_specs=whole((blocks, packet, LANES)),
        scratch_shapes=[pltpu.VMEM((2, tall, LANES), F32)],
    )(
        positions,
        query_input,
        output_gradient,
        key_input,
        value_input,
        log_softmax_norm,
        output_delta_rows,
    )
    packed = lax.all_to_all(packed, "ctx", split_axis=0, concat_axis=0, tiled=True)
    sent = jax.ShapeDtypeStruct((tokens + rows, LANES), BF16)
    own, *sends = pl.pallas_call(
        spread_kernel,
        name="spread",
        grid=(1,),
        out_shape=[jax.ShapeDtypeStruct((rows, LANES), BF16)] + [sent] * (planes - 1),
        in_specs=[pl.BlockSpec((blocks, 2 * rows, LANES), lambda i: (0, group // 2, 0))],
        out_specs=[pl.BlockSpec((rows, LANES), lambda i: (0, 0))]
        + [pl.BlockSpec((tokens + rows, LANES), lambda i: (0, 0))] * (planes - 1),
    )(packed)

    def swap(array, by):
        return lax.ppermute(array, "head", [(i, i ^ by) for i in range(planes)])

    got = [swap(sends[j - 1], j) for j in range(1, planes)]
    part = jax.ShapeDtypeStruct((tokens, LANES), BF16)
    packet = (group // 2 + 1) * rows
    back, total, *parts = pl.pallas_call(
        make_attend(planes),
        name="attend",
        out_shape=[
            jax.ShapeDtypeStruct((blocks, packet, LANES), BF16),
            jax.ShapeDtypeStruct((tokens, LANES), F32),
        ]
        + [part] * (planes - 1),
        in_specs=[whole(packed.shape), whole(own.shape)] + [whole(g.shape) for g in got],
        out_specs=[whole((blocks, packet, LANES)), whole((tokens, LANES))]
        + [whole((tokens, LANES))] * (planes - 1),
        scratch_shapes=[
            pltpu.VMEM((tokens, 2 * LANES), BF16),
            pltpu.VMEM((group, 2 * tokens, 2 * LANES), BF16),
            pltpu.VMEM((group * tokens, LANES), BF16),
            pltpu.VMEM((tokens, group * tokens), BF16),
            pltpu.VMEM((tokens, group * tokens), BF16),
        ],
    )(packed, own, *got)
    parts = [swap(parts[j - 1], j) for j in range(1, planes)]
    last = pl.BlockSpec((blocks, rows, LANES), lambda i: (0, group // 2, 0))
    flat = pl.BlockSpec((tokens, LANES), lambda i: (0, 0))
    back = pl.pallas_call(
        total_kernel,
        name="total",
        grid=(1,),
        out_shape=jax.ShapeDtypeStruct(back.shape, BF16),
        in_specs=[flat] * planes + [pl.BlockSpec(memory_space=pl.ANY)],
        out_specs=last,
        input_output_aliases={planes: 0},
    )(total, *parts, back)
    back = lax.all_to_all(back, "ctx", split_axis=0, concat_axis=0, tiled=True)
    shapes = [query_input.shape, key_input.shape, value_input.shape]
    return tuple(
        pl.pallas_call(
            unpack_kernel,
            name="unpack",
            out_shape=[jax.ShapeDtypeStruct(s, BF16) for s in shapes],
            in_specs=[whole(back.shape)],
            out_specs=[whole(s) for s in shapes],
        )(back)
    )


def solution(mesh):
    def on_each(*args):
        query_input, key_input = args[0], args[1]
        kv_heads = key_input.shape[1] // HEAD_WIDTH
        group = query_input.shape[1] // key_input.shape[1]
        blocks, planes = mesh.shape["ctx"], mesh.shape["head"]
        by_head = (
            blocks == kv_heads
            and group == 4
            and planes == 4
            and kv_heads == 8
            and query_input.shape[0] % 16 == 0
        )
        return (by_heads if by_head else on_device)(*args)

    return jax.shard_map(
        on_each,
        mesh=mesh,
        in_specs=(
            P(("ctx", "head"), None),
            P(("ctx", "head"), None),
            P(("ctx", "head"), None),
            P(("ctx", "head"), None),
            P("ctx", "head"),
            P("ctx", "head"),
            P("ctx"),
        ),
        out_specs=(P(("ctx", "head"), None), P(("ctx", "head"), None), P(("ctx", "head"), None)),
        check_vma=False,
    )
```

```python
import jax
import jax.numpy as jnp
from jax import lax
from jax.experimental import pallas as pl
from jax.experimental.pallas import tpu as pltpu
from jax.sharding import PartitionSpec as P

HEAD_WIDTH = 64
LANES = 128
PIECES = 2
MASKED = 16384.0
F32 = jnp.float32
BF16 = jnp.bfloat16


def for_sending(array):
    return jax.tree.map(lambda a: a.astype(jnp.bfloat16) if a.dtype == jnp.float32 else a, array)


def from_behind(array, axis, by):
    count = lax.axis_size(axis)
    return lax.ppermute(array, axis, [(i, (i + by) % count) for i in range(count)])


def block_terms(
    query, grad_rows, norm_rows, delta_part, query_pos, key_block, value_block, key_pos
):
    row_count = query.shape[0]
    col_count = key_block.shape[0]
    kv_heads = key_block.shape[1] // HEAD_WIDTH
    query_group_width = query.shape[1] // (kv_heads * HEAD_WIDTH)
    score_scale = HEAD_WIDTH ** (-0.5)
    query_per_head = query.reshape(row_count, kv_heads, query_group_width, HEAD_WIDTH)
    gradient_per_head = grad_rows.reshape(row_count, kv_heads, query_group_width, HEAD_WIDTH)
    key_per_head = key_block.reshape(col_count, kv_heads, HEAD_WIDTH)
    value_per_head = value_block.reshape(col_count, kv_heads, HEAD_WIDTH)
    scores = (
        jnp.einsum(
            "qhgd,khd->qhgk", query_per_head, key_per_head, preferred_element_type=jnp.float32
        )
        * score_scale
    )
    visible = (query_pos[:, None] >= key_pos[None, :])[:, None, None, :]
    norm_cols = norm_rows.reshape(row_count, kv_heads, query_group_width, 1)
    probabilities = jnp.where(visible, jnp.exp(scores - norm_cols), 0.0)
    grad_prob = jnp.einsum(
        "qhgd,khd->qhgk", gradient_per_head, value_per_head, preferred_element_type=jnp.float32
    )
    grad_score = probabilities * (
        grad_prob - delta_part.reshape(row_count, kv_heads, query_group_width, 1)
    )
    prob_rounded = probabilities.astype(jnp.bfloat16)
    score_rounded = grad_score.astype(jnp.bfloat16)
    value_term = jnp.einsum(
        "qhgk,qhgd->khd", prob_rounded, gradient_per_head, preferred_element_type=jnp.float32
    )
    key_term = score_scale * jnp.einsum(
        "qhgk,qhgd->khd", score_rounded, query_per_head, preferred_element_type=jnp.float32
    )
    query_term = score_scale * jnp.einsum(
        "qhgk,khd->qhgd", score_rounded, key_per_head, preferred_element_type=jnp.float32
    )
    return (
        query_term.reshape(row_count, -1),
        key_term.reshape(col_count, -1),
        value_term.reshape(col_count, -1),
    )


def no_terms(operands):
    query = operands[0]
    key_block = operands[5]
    return (
        jnp.zeros(query.shape, jnp.float32),
        jnp.zeros(key_block.shape, jnp.float32),
        jnp.zeros(key_block.shape, jnp.float32),
    )


def all_terms(operands):
    return block_terms(*operands)


def pair_terms(query, grad_rows, norm_rows, delta_part, query_pos, key_block, value_block, key_pos):
    row_half = query.shape[0] // 2
    col_half = key_block.shape[0] // 2
    zero_cols = jnp.zeros((col_half, key_block.shape[1]), jnp.float32)
    key_sums = [zero_cols, zero_cols]
    value_sums = [zero_cols, zero_cols]
    query_parts = []
    for row_side in range(2):
        rows_here = slice(row_side * row_half, (row_side + 1) * row_half)
        query_sum = jnp.zeros((row_half, query.shape[1]), jnp.float32)
        for col_side in range(2):
            cols_here = slice(col_side * col_half, (col_side + 1) * col_half)
            operands = (
                query[rows_here],
                grad_rows[rows_here],
                norm_rows[rows_here],
                delta_part[rows_here],
                query_pos[rows_here],
                key_block[cols_here],
                value_block[cols_here],
                key_pos[cols_here],
            )
            reached = jnp.any(query_pos[rows_here][:, None] >= key_pos[cols_here][None, :])
            query_term, key_term, value_term = lax.cond(reached, all_terms, no_terms, operands)
            query_sum = query_sum + query_term
            key_sums[col_side] = key_sums[col_side] + key_term
            value_sums[col_side] = value_sums[col_side] + value_term
        query_parts.append(query_sum)
    return (
        jnp.concatenate(query_parts, 0),
        jnp.concatenate(key_sums, 0),
        jnp.concatenate(value_sums, 0),
    )


def pass_keys(traveler, offset):
    return from_behind((for_sending(traveler[0]), for_sending(traveler[1])), "ctx", offset)


def pass_sums(traveler, offset):
    return from_behind((traveler[2], traveler[3], traveler[4]), "ctx", offset)


def on_device(
    query_input,
    key_input,
    value_input,
    output_gradient,
    log_softmax_norm,
    output_delta_rows,
    positions,
):
    query, key_local, value_local, grad_rows = (
        lax.all_to_all(query_input, "head", split_axis=1, concat_axis=0, tiled=True),
        lax.all_to_all(key_input, "head", split_axis=1, concat_axis=0, tiled=True),
        lax.all_to_all(value_input, "head", split_axis=1, concat_axis=0, tiled=True),
        lax.all_to_all(output_gradient, "head", split_axis=1, concat_axis=0, tiled=True),
    )
    query_pos = positions.astype(jnp.float32)
    row_count = query.shape[0]
    feature_width = key_local.shape[1]
    grad_query = jnp.zeros(query.shape, jnp.float32)

    def visit(key_block, value_block, key_pos):
        return pair_terms(
            query,
            grad_rows,
            log_softmax_norm,
            output_delta_rows,
            query_pos,
            key_block,
            value_block,
            key_pos,
        )

    offsets = (1,)
    bounds = ((0, row_count),)
    travelers = tuple(
        (
            (
                key_local,
                value_local,
                jnp.zeros((upper_row - lower_row, feature_width), jnp.float32),
                jnp.zeros((upper_row - lower_row, feature_width), jnp.float32),
                query_pos,
            )
            for lower_row, upper_row in bounds
        )
    )

    def absorb_all(query_sum, travelers):
        updated = []
        for traveler in travelers:
            key_block, value_block, key_acc, value_acc, key_pos = traveler
            query_term, key_term, value_term = visit(key_block, value_block, key_pos)
            query_sum = query_sum + query_term
            updated.append(
                (key_block, value_block, key_acc + key_term, value_acc + value_term, key_pos)
            )
        return (query_sum, tuple(updated))

    def cycle_turn(turn_index, running):
        query_sum, travelers = absorb_all(running[0], running[1])
        moved = []
        for traveler, offset in zip(travelers, offsets):
            key_block, value_block = pass_keys(traveler, offset)
            key_acc, value_acc, key_pos = pass_sums(traveler, offset)
            moved.append((key_block, value_block, key_acc, value_acc, key_pos))
        return (query_sum, tuple(moved))

    grad_query, travelers = lax.fori_loop(
        0, lax.axis_size("ctx") - 1, cycle_turn, (grad_query, travelers)
    )
    grad_query, travelers = absorb_all(grad_query, travelers)
    returned = [pass_sums(traveler, offset) for traveler, offset in zip(travelers, offsets)]
    key_gradient = jnp.concatenate([arrived[0] for arrived in returned], 0)
    value_gradient = jnp.concatenate([arrived[1] for arrived in returned], 0)
    query_out, key_out, value_out = (
        lax.all_to_all(
            grad_query.astype(jnp.bfloat16), "head", split_axis=0, concat_axis=1, tiled=True
        ),
        lax.all_to_all(
            key_gradient.astype(jnp.bfloat16), "head", split_axis=0, concat_axis=1, tiled=True
        ),
        lax.all_to_all(
            value_gradient.astype(jnp.bfloat16), "head", split_axis=0, concat_axis=1, tiled=True
        ),
    )
    return (query_out, key_out, value_out)


def lane_of(shape):
    return lax.broadcasted_iota(jnp.int32, shape, len(shape) - 1)


def pack_kernel(*refs):
    sources, out_ref, near, wide_ref, sems = refs[:7], refs[7], refs[8:15], refs[15], refs[16]
    pos_ref, q_ref, g_ref, k_ref, v_ref, n_ref, d_ref = near
    copies = [
        pltpu.make_async_copy(source, target, sems.at[i])
        for i, (source, target) in enumerate(zip(sources, near))
    ]
    for i in (1, 2, 3, 4, 5, 6, 0):
        copies[i].start()
    copies[1].wait()
    copies[2].wait()
    rows = q_ref.shape[0]
    tall = pos_ref.shape[0]
    planes = tall // rows
    block = lax.axis_index("ctx")
    kv_heads = out_ref.shape[0]
    group = q_ref.shape[1] // k_ref.shape[1]
    lane = lane_of((rows, LANES))
    low = lane < HEAD_WIDTH
    scale = HEAD_WIDTH ** (-0.5)
    for m in range(q_ref.shape[1] // LANES):
        cols = slice(m * LANES, (m + 1) * LANES)
        q = q_ref[:, cols].astype(F32) * scale
        g = g_ref[:, cols].astype(F32)
        c, e = (2 * m) // group, (2 * m) % group
        even = jnp.where(low, q, pltpu.roll(g, HEAD_WIDTH, 1))
        odd = jnp.where(low, pltpu.roll(q, HEAD_WIDTH, 1), g)
        out_ref[c, e * rows : (e + 1) * rows, :] = even.astype(BF16)
        out_ref[c, (e + 1) * rows : (e + 2) * rows, :] = odd.astype(BF16)
    at = group * rows
    copies[3].wait()
    copies[4].wait()
    for m in range(k_ref.shape[1] // LANES):
        cols = slice(m * LANES, (m + 1) * LANES)
        k = k_ref[:, cols].astype(F32)
        v = v_ref[:, cols].astype(F32)
        even = jnp.where(low, k, pltpu.roll(v, HEAD_WIDTH, 1))
        odd = jnp.where(low, pltpu.roll(k, HEAD_WIDTH, 1), v)
        out_ref[2 * m, at : at + rows, :] = even.astype(BF16)
        out_ref[2 * m + 1, at : at + rows, :] = odd.astype(BF16)
    at = at + rows
    copies[5].wait()
    copies[6].wait()
    copies[0].wait()
    wide_ref[...] = jnp.zeros(wide_ref.shape, F32)
    wide_ref[0, 0 : n_ref.shape[0], :] = n_ref[...]
    wide_ref[1, 0 : d_ref.shape[0], :] = d_ref[...]
    tall_lane = lane_of((tall, LANES))
    row_half = tall // 2
    lead = (pos_ref[0] // row_half).astype(F32)
    for parity in range(2):
        spread = jnp.zeros((tall, LANES), F32)
        for t in range(2):
            rest = wide_ref[t].T
            for s in range(PIECES):
                piece = rest.astype(BF16).astype(F32)
                rest = rest - piece
                to = s * 2 * group + t * group
                here = (tall_lane >= to) & (tall_lane < to + group)
                moved = pltpu.roll(piece, (to - group * parity) % LANES, 1)
                spread = jnp.where(here, moved, spread)
        width = PIECES * 2 * group
        tile = jnp.zeros((rows, LANES), F32)
        for h in range(planes):
            part = spread[h * rows : (h + 1) * rows]
            moved = pltpu.roll(part, h * width, 1) if h else part
            tile = jnp.where((lane >= h * width) & (lane < (h + 1) * width), moved, tile)
        first = planes * width
        mine = (lane >= first) & (lane < first + planes * kv_heads) & (lane % kv_heads == block)
        tile = jnp.where(mine, lead, tile).astype(BF16)
        for c in range(parity, kv_heads, 2):
            out_ref[c, at : at + rows, :] = tile


def spread_kernel(in_ref, own_ref, *send_refs):
    blocks, packet, _ = in_ref.shape
    rows = own_ref.shape[0]
    plane = lax.axis_index("head")
    width = LANES // blocks
    lane = lane_of((rows, LANES))
    kv = in_ref[:, packet - 2 * rows : packet - rows, :].reshape(blocks * rows, LANES)
    tiles = [in_ref[b, packet - rows : packet, :].astype(F32) for b in range(blocks)]
    for j in range(len(send_refs) + 1):
        wanted = plane ^ j
        tile = jnp.zeros((rows, LANES), F32)
        for b in range(blocks):
            shift = lax.rem(b * width - wanted * width + LANES, LANES)
            here = (lane >= b * width) & (lane < (b + 1) * width)
            tile = jnp.where(here, pltpu.roll(tiles[b], shift, 1), tile)
        if j == 0:
            own_ref[...] = tile.astype(BF16)
        else:
            send_refs[j - 1][0 : blocks * rows, :] = kv
            send_refs[j - 1][blocks * rows : (blocks + 1) * rows, :] = tile.astype(BF16)


def make_attend_others(planes):
    def attend_others_kernel(in_ref, own_ref, *refs):
        got = refs[: planes - 1]
        send_refs = refs[planes - 1 : 2 * planes - 2]
        right_ref, both_ref, scores_ref, query_ref, left_ref, prob_ref = refs[2 * planes - 2 :]
        blocks = in_ref.shape[0]
        rows = own_ref.shape[0]
        group = in_ref.shape[1] // rows - 2
        tokens = blocks * rows
        width = LANES // blocks
        plane = lax.axis_index("head")
        holder = plane ^ (lax.axis_index("ctx") // (blocks // planes))
        lane = lane_of((rows, LANES))
        lane_row = lane_of((1, LANES))
        first = planes * width

        tile = own_ref[...].astype(F32)
        for j in range(1, planes):
            other = got[j - 1][tokens : tokens + rows, :].astype(F32)
            tile = jnp.where(holder == j, other, tile)
        folds = (tile, pltpu.roll(tile, LANES // 2, 1))

        lead = jnp.zeros((1, LANES), F32)
        for b in range(blocks):
            at = (group + 1) * rows
            lead = lead + in_ref[b, at : at + rows, :].astype(F32)[0:1]
        key_plane = (lane_row - first) // blocks
        per_half = planes // 2
        count = 2 * blocks

        def place(lead_of, which):
            front = per_half * lead_of + which
            back = per_half * (count - 1 - lead_of) + (which - per_half)
            return jnp.where(which < per_half, front, back)

        key_place = place(lead, key_plane.astype(F32))
        in_mask = (lane_row >= first) & (lane_row < first + planes * blocks)

        low = lane_of((tokens, LANES)) < HEAD_WIDTH
        nothing = jnp.zeros((tokens, LANES), BF16)
        for e in range(group):
            pair = in_ref[:, e * rows : (e + 1) * rows, :].reshape(tokens, LANES)
            both_ref[e * tokens : (e + 1) * tokens, :] = pair
            right_ref[e, 0:tokens, 0:LANES] = jnp.where(low, pair, nothing)
            right_ref[e, tokens : 2 * tokens, 0:LANES] = jnp.where(low, nothing, pair)
        for b in range(blocks):
            lead_b = jnp.sum(
                jnp.where(lane_row == first + b, lead, 0.0), axis=1, keepdims=True
            )
            query_place = place(lead_b, plane.astype(F32))
            hidden = jnp.where(in_mask & (key_place > query_place), MASKED, 0.0)
            fold = folds[(b * width) // (LANES // 2)]
            at = (b * width) % (LANES // 2)
            near = (lane >= at) & (lane < at + width)
            for e in range(group):
                norm = jnp.where(near & (lane % (2 * group) == e), fold, hidden)
                delta = jnp.where(near & (lane % (2 * group) == group + e), fold, 0.0)
                down = slice(b * rows, (b + 1) * rows)
                right_ref[e, down, LANES:] = norm.astype(BF16)
                down = slice(tokens + b * rows, tokens + (b + 1) * rows)
                right_ref[e, down, LANES:] = delta.astype(BF16)

        for j in range(1, planes):
            kv = got[j - 1][0:tokens, :]
            scores_here = scores_ref.at[(j - 1) * tokens : j * tokens]
            kv_sum = pair_sums(
                kv, first + (plane ^ j) * blocks, first, rows, None,
                left_ref, right_ref, both_ref, prob_ref, scores_here,
            )
            send_refs[j - 1][...] = kv_sum.astype(BF16)
            query_ref[j - 1] = kv

    return attend_others_kernel


def pair_sums(
    kv, mark_from, first, rows, allowed, left_ref, right_ref, both_ref, prob_ref, score_ref
):
    tokens = kv.shape[0]
    group = right_ref.shape[0]
    key_row = lax.broadcasted_iota(jnp.int32, (tokens, LANES), 0)
    wide_lane = lane_of((tokens, LANES))
    low = wide_lane < HEAD_WIDTH
    mark = mark_from + key_row // rows
    ones = jnp.where((wide_lane < first) | (wide_lane == mark), -1.0, 0.0)
    left_ref[:, 0:LANES] = kv
    left_ref[:, LANES:] = ones.astype(BF16)
    for e in range(group):
        both = lax.dot_general(
            left_ref[...],
            right_ref[e],
            (((1,), (1,)), ((), ())),
            preferred_element_type=F32,
        )
        prob = jnp.exp(both[:, 0:tokens])
        if allowed is not None:
            prob = jnp.where(allowed, prob, 0.0)
        score = prob * both[:, tokens:]
        across = slice(e * tokens, (e + 1) * tokens)
        prob_ref[:, across] = prob.astype(BF16)
        score_ref[:, across] = score.astype(BF16)
    value_side = jnp.dot(prob_ref[...], both_ref[...], preferred_element_type=F32)
    key_side = jnp.dot(score_ref[...], both_ref[...], preferred_element_type=F32)
    return jnp.where(low, key_side, value_side)


def attend_own_kernel(
    in_ref, right_ref, both_ref, scores_ref, keys_ref, out_ref, sum_ref, left_ref, prob_ref, score_ref
):
    others, tokens, _ = keys_ref.shape
    blocks = in_ref.shape[0]
    rows = tokens // blocks
    group = right_ref.shape[0]
    plane = lax.axis_index("head")
    planes = others + 1
    first = planes * (LANES // blocks)
    square_key = lax.broadcasted_iota(jnp.int32, (tokens, tokens), 0)
    square_query = lane_of((tokens, tokens))
    allowed = (square_key <= square_query) | (square_key // rows != square_query // rows)
    kv = in_ref[:, group * rows : (group + 1) * rows, :].reshape(tokens, LANES)
    sum_ref[...] = pair_sums(
        kv, first + plane * blocks, first, rows, allowed,
        left_ref, right_ref, both_ref, prob_ref, score_ref,
    )
    turned = kv.astype(F32).T[0:HEAD_WIDTH].astype(BF16)
    query_sum = jnp.dot(turned, score_ref[...], preferred_element_type=F32)
    for j in range(others):
        turned = keys_ref[j].astype(F32).T[0:HEAD_WIDTH].astype(BF16)
        query_sum = query_sum + jnp.dot(
            turned, scores_ref[j * tokens : (j + 1) * tokens, :], preferred_element_type=F32
        )
    scale = HEAD_WIDTH ** (-0.5)
    for m in range(group // 2):
        pair = jnp.concatenate(
            [
                query_sum[:, 2 * m * tokens : (2 * m + 1) * tokens],
                query_sum[:, (2 * m + 1) * tokens : (2 * m + 2) * tokens],
            ],
            0,
        )
        done = (pair.T * scale).astype(BF16)
        out_ref[:, m * rows : (m + 1) * rows, :] = done.reshape(blocks, rows, LANES)


def total_kernel(sum_ref, *refs):
    got, out_ref = refs[:-2], refs[-1]
    total = sum_ref[...]
    for ref in got:
        total = total + ref[...].astype(F32)
    out_ref[...] = total.astype(BF16).reshape(out_ref.shape)


def unpack_kernel(in_ref, q_ref, k_ref, v_ref):
    rows = q_ref.shape[0]
    heads = in_ref.shape[0]
    tiles = in_ref.shape[1] // rows - 1
    low = lane_of((rows, LANES)) < HEAD_WIDTH
    for c in range(heads):
        for m in range(tiles):
            at = (c * tiles + m) * LANES
            q_ref[:, at : at + LANES] = in_ref[c, m * rows : (m + 1) * rows, :]
    for m in range(heads // 2):
        even = in_ref[2 * m, tiles * rows : (tiles + 1) * rows, :].astype(F32)
        odd = in_ref[2 * m + 1, tiles * rows : (tiles + 1) * rows, :].astype(F32)
        cols = slice(m * LANES, (m + 1) * LANES)
        k_ref[:, cols] = jnp.where(low, even, pltpu.roll(odd, HEAD_WIDTH, 1)).astype(BF16)
        v_ref[:, cols] = jnp.where(low, pltpu.roll(even, HEAD_WIDTH, 1), odd).astype(BF16)


def whole(shape):
    return pl.BlockSpec(shape, lambda: (0,) * len(shape))


ROOMY = pltpu.CompilerParams(vmem_limit_bytes=24 << 20)
KEPT = pl.BlockSpec(memory_space=pltpu.VMEM)


def kept(*arrays):
    return [pltpu.with_memory_space_constraint(a, pltpu.VMEM) for a in arrays]


def by_heads(
    query_input,
    key_input,
    value_input,
    output_gradient,
    log_softmax_norm,
    output_delta_rows,
    positions,
):
    blocks = lax.axis_size("ctx")
    planes = lax.axis_size("head")
    rows = query_input.shape[0]
    tokens = blocks * rows
    group = query_input.shape[1] // key_input.shape[1]
    packet = (group + 2) * rows
    tall = positions.shape[0]
    norm_cols, delta_cols = log_softmax_norm.T, output_delta_rows.T
    arguments = (
        positions,
        query_input,
        output_gradient,
        key_input,
        value_input,
        norm_cols,
        delta_cols,
    )
    packed = pl.pallas_call(
        pack_kernel,
        name="pack",
        compiler_params=ROOMY,
        out_shape=pltpu.VMEM((blocks, packet, LANES), BF16),
        in_specs=[pl.BlockSpec(memory_space=pl.ANY)] * len(arguments),
        out_specs=KEPT,
        scratch_shapes=[
            pltpu.SMEM(a.shape, a.dtype) if a.ndim == 1 else pltpu.VMEM(a.shape, a.dtype)
            for a in arguments
        ]
        + [pltpu.VMEM((2, LANES, tall), F32), pltpu.SemaphoreType.DMA((len(arguments),))],
    )(*[pltpu.with_memory_space_constraint(a, pltpu.HBM) for a in arguments])
    packed = lax.all_to_all(packed, "ctx", split_axis=0, concat_axis=0, tiled=True)
    (packed,) = kept(packed)
    own, *sends = pl.pallas_call(
        spread_kernel,
        name="spread",
        compiler_params=ROOMY,
        out_shape=[pltpu.VMEM((rows, LANES), BF16)]
        + [pltpu.VMEM((tokens + rows, LANES), BF16)] * (planes - 1),
        in_specs=[KEPT],
        out_specs=[KEPT] * planes,
    )(packed)

    def swap(array, by):
        return lax.ppermute(array, "head", [(i, i ^ by) for i in range(planes)])

    got = [swap(sends[j - 1], j) for j in range(1, planes)]
    wide = group * tokens
    *parts, right, both, scores, keys = pl.pallas_call(
        make_attend_others(planes),
        name="attend_others",
        compiler_params=ROOMY,
        out_shape=[pltpu.VMEM((tokens, LANES), BF16)] * (planes - 1)
        + [
            pltpu.VMEM((group, 2 * tokens, 2 * LANES), BF16),
            pltpu.VMEM((wide, LANES), BF16),
            pltpu.VMEM(((planes - 1) * tokens, wide), BF16),
            pltpu.VMEM((planes - 1, tokens, LANES), BF16),
        ],
        in_specs=[KEPT] * (planes + 1),
        out_specs=[KEPT] * (planes + 3),
        scratch_shapes=[
            pltpu.VMEM((tokens, 2 * LANES), BF16),
            pltpu.VMEM((tokens, wide), BF16),
        ],
    )(*kept(packed, own, *got))
    parts = [swap(parts[j - 1], j) for j in range(1, planes)]
    packet = (group // 2 + 1) * rows
    back, total = pl.pallas_call(
        attend_own_kernel,
        name="attend_own",
        compiler_params=ROOMY,
        out_shape=[
            jax.ShapeDtypeStruct((blocks, packet, LANES), BF16),
            pltpu.VMEM((tokens, LANES), F32),
        ],
        in_specs=[KEPT] * 5,
        out_specs=[whole((blocks, packet, LANES)), KEPT],
        scratch_shapes=[
            pltpu.VMEM((tokens, 2 * LANES), BF16),
            pltpu.VMEM((tokens, wide), BF16),
            pltpu.VMEM((tokens, wide), BF16),
        ],
        cost_estimate=pl.CostEstimate(
            flops=4 * wide * tokens * LANES * 4, transcendentals=wide * tokens, bytes_accessed=1 << 22
        ),
    )(*kept(packed, right, both, scores, keys))
    last = pl.BlockSpec((blocks, rows, LANES), lambda i: (0, group // 2, 0))
    back = pl.pallas_call(
        total_kernel,
        name="total",
        compiler_params=ROOMY,
        grid=(1,),
        out_shape=jax.ShapeDtypeStruct(back.shape, BF16),
        in_specs=[KEPT] * planes + [pl.BlockSpec(memory_space=pl.ANY)],
        out_specs=last,
        input_output_aliases={planes: 0},
    )(*kept(total, *parts), back)
    back = lax.all_to_all(back, "ctx", split_axis=0, concat_axis=0, tiled=True)
    (back,) = kept(back)
    shapes = [query_input.shape, key_input.shape, value_input.shape]
    return tuple(
        pl.pallas_call(
            unpack_kernel,
            name="unpack",
        compiler_params=ROOMY,
            out_shape=[jax.ShapeDtypeStruct(s, BF16) for s in shapes],
            in_specs=[KEPT],
            out_specs=[whole(s) for s in shapes],
        )(back)
    )


def solution(mesh):
    def on_each(*args):
        query_input, key_input = args[0], args[1]
        kv_heads = key_input.shape[1] // HEAD_WIDTH
        group = query_input.shape[1] // key_input.shape[1]
        blocks, planes = mesh.shape["ctx"], mesh.shape["head"]
        by_head = (
            blocks == kv_heads
            and group == 4
            and planes == 4
            and kv_heads == 8
            and query_input.shape[0] % 16 == 0
        )
        return (by_heads if by_head else on_device)(*args)

    return jax.shard_map(
        on_each,
        mesh=mesh,
        in_specs=(
            P(("ctx", "head"), None),
            P(("ctx", "head"), None),
            P(("ctx", "head"), None),
            P(("ctx", "head"), None),
            P("ctx", "head"),
            P("ctx", "head"),
            P("ctx"),
        ),
        out_specs=(P(("ctx", "head"), None), P(("ctx", "head"), None), P(("ctx", "head"), None)),
        check_vma=False,
    )
```

```python
import jax
import jax.numpy as jnp
from jax import lax
from jax.experimental import pallas as pl
from jax.experimental.pallas import tpu as pltpu
from jax.sharding import PartitionSpec as P

HEAD_WIDTH = 64
LANES = 128
PIECES = 2
ORDER = (2, 3, 1)
MASKED = 16384.0
F32 = jnp.float32
BF16 = jnp.bfloat16


def for_sending(array):
    return jax.tree.map(lambda a: a.astype(jnp.bfloat16) if a.dtype == jnp.float32 else a, array)


def from_behind(array, axis, by):
    count = lax.axis_size(axis)
    return lax.ppermute(array, axis, [(i, (i + by) % count) for i in range(count)])


def block_terms(
    query, grad_rows, norm_rows, delta_part, query_pos, key_block, value_block, key_pos
):
    row_count = query.shape[0]
    col_count = key_block.shape[0]
    kv_heads = key_block.shape[1] // HEAD_WIDTH
    query_group_width = query.shape[1] // (kv_heads * HEAD_WIDTH)
    score_scale = HEAD_WIDTH ** (-0.5)
    query_per_head = query.reshape(row_count, kv_heads, query_group_width, HEAD_WIDTH)
    gradient_per_head = grad_rows.reshape(row_count, kv_heads, query_group_width, HEAD_WIDTH)
    key_per_head = key_block.reshape(col_count, kv_heads, HEAD_WIDTH)
    value_per_head = value_block.reshape(col_count, kv_heads, HEAD_WIDTH)
    scores = (
        jnp.einsum(
            "qhgd,khd->qhgk", query_per_head, key_per_head, preferred_element_type=jnp.float32
        )
        * score_scale
    )
    visible = (query_pos[:, None] >= key_pos[None, :])[:, None, None, :]
    norm_cols = norm_rows.reshape(row_count, kv_heads, query_group_width, 1)
    probabilities = jnp.where(visible, jnp.exp(scores - norm_cols), 0.0)
    grad_prob = jnp.einsum(
        "qhgd,khd->qhgk", gradient_per_head, value_per_head, preferred_element_type=jnp.float32
    )
    grad_score = probabilities * (
        grad_prob - delta_part.reshape(row_count, kv_heads, query_group_width, 1)
    )
    prob_rounded = probabilities.astype(jnp.bfloat16)
    score_rounded = grad_score.astype(jnp.bfloat16)
    value_term = jnp.einsum(
        "qhgk,qhgd->khd", prob_rounded, gradient_per_head, preferred_element_type=jnp.float32
    )
    key_term = score_scale * jnp.einsum(
        "qhgk,qhgd->khd", score_rounded, query_per_head, preferred_element_type=jnp.float32
    )
    query_term = score_scale * jnp.einsum(
        "qhgk,khd->qhgd", score_rounded, key_per_head, preferred_element_type=jnp.float32
    )
    return (
        query_term.reshape(row_count, -1),
        key_term.reshape(col_count, -1),
        value_term.reshape(col_count, -1),
    )


def no_terms(operands):
    query = operands[0]
    key_block = operands[5]
    return (
        jnp.zeros(query.shape, jnp.float32),
        jnp.zeros(key_block.shape, jnp.float32),
        jnp.zeros(key_block.shape, jnp.float32),
    )


def all_terms(operands):
    return block_terms(*operands)


def pair_terms(query, grad_rows, norm_rows, delta_part, query_pos, key_block, value_block, key_pos):
    row_half = query.shape[0] // 2
    col_half = key_block.shape[0] // 2
    zero_cols = jnp.zeros((col_half, key_block.shape[1]), jnp.float32)
    key_sums = [zero_cols, zero_cols]
    value_sums = [zero_cols, zero_cols]
    query_parts = []
    for row_side in range(2):
        rows_here = slice(row_side * row_half, (row_side + 1) * row_half)
        query_sum = jnp.zeros((row_half, query.shape[1]), jnp.float32)
        for col_side in range(2):
            cols_here = slice(col_side * col_half, (col_side + 1) * col_half)
            operands = (
                query[rows_here],
                grad_rows[rows_here],
                norm_rows[rows_here],
                delta_part[rows_here],
                query_pos[rows_here],
                key_block[cols_here],
                value_block[cols_here],
                key_pos[cols_here],
            )
            reached = jnp.any(query_pos[rows_here][:, None] >= key_pos[cols_here][None, :])
            query_term, key_term, value_term = lax.cond(reached, all_terms, no_terms, operands)
            query_sum = query_sum + query_term
            key_sums[col_side] = key_sums[col_side] + key_term
            value_sums[col_side] = value_sums[col_side] + value_term
        query_parts.append(query_sum)
    return (
        jnp.concatenate(query_parts, 0),
        jnp.concatenate(key_sums, 0),
        jnp.concatenate(value_sums, 0),
    )


def pass_keys(traveler, offset):
    return from_behind((for_sending(traveler[0]), for_sending(traveler[1])), "ctx", offset)


def pass_sums(traveler, offset):
    return from_behind((traveler[2], traveler[3], traveler[4]), "ctx", offset)


def on_device(
    query_input,
    key_input,
    value_input,
    output_gradient,
    log_softmax_norm,
    output_delta_rows,
    positions,
):
    query, key_local, value_local, grad_rows = (
        lax.all_to_all(query_input, "head", split_axis=1, concat_axis=0, tiled=True),
        lax.all_to_all(key_input, "head", split_axis=1, concat_axis=0, tiled=True),
        lax.all_to_all(value_input, "head", split_axis=1, concat_axis=0, tiled=True),
        lax.all_to_all(output_gradient, "head", split_axis=1, concat_axis=0, tiled=True),
    )
    query_pos = positions.astype(jnp.float32)
    row_count = query.shape[0]
    feature_width = key_local.shape[1]
    grad_query = jnp.zeros(query.shape, jnp.float32)

    def visit(key_block, value_block, key_pos):
        return pair_terms(
            query,
            grad_rows,
            log_softmax_norm,
            output_delta_rows,
            query_pos,
            key_block,
            value_block,
            key_pos,
        )

    offsets = (1,)
    bounds = ((0, row_count),)
    travelers = tuple(
        (
            (
                key_local,
                value_local,
                jnp.zeros((upper_row - lower_row, feature_width), jnp.float32),
                jnp.zeros((upper_row - lower_row, feature_width), jnp.float32),
                query_pos,
            )
            for lower_row, upper_row in bounds
        )
    )

    def absorb_all(query_sum, travelers):
        updated = []
        for traveler in travelers:
            key_block, value_block, key_acc, value_acc, key_pos = traveler
            query_term, key_term, value_term = visit(key_block, value_block, key_pos)
            query_sum = query_sum + query_term
            updated.append(
                (key_block, value_block, key_acc + key_term, value_acc + value_term, key_pos)
            )
        return (query_sum, tuple(updated))

    def cycle_turn(turn_index, running):
        query_sum, travelers = absorb_all(running[0], running[1])
        moved = []
        for traveler, offset in zip(travelers, offsets):
            key_block, value_block = pass_keys(traveler, offset)
            key_acc, value_acc, key_pos = pass_sums(traveler, offset)
            moved.append((key_block, value_block, key_acc, value_acc, key_pos))
        return (query_sum, tuple(moved))

    grad_query, travelers = lax.fori_loop(
        0, lax.axis_size("ctx") - 1, cycle_turn, (grad_query, travelers)
    )
    grad_query, travelers = absorb_all(grad_query, travelers)
    returned = [pass_sums(traveler, offset) for traveler, offset in zip(travelers, offsets)]
    key_gradient = jnp.concatenate([arrived[0] for arrived in returned], 0)
    value_gradient = jnp.concatenate([arrived[1] for arrived in returned], 0)
    query_out, key_out, value_out = (
        lax.all_to_all(
            grad_query.astype(jnp.bfloat16), "head", split_axis=0, concat_axis=1, tiled=True
        ),
        lax.all_to_all(
            key_gradient.astype(jnp.bfloat16), "head", split_axis=0, concat_axis=1, tiled=True
        ),
        lax.all_to_all(
            value_gradient.astype(jnp.bfloat16), "head", split_axis=0, concat_axis=1, tiled=True
        ),
    )
    return (query_out, key_out, value_out)


def lane_of(shape):
    return lax.broadcasted_iota(jnp.int32, shape, len(shape) - 1)


def slots_of(near_refs, far_refs):
    packet = near_refs[0].shape[1]
    views = [ref.at[0] for ref in near_refs]
    for ref in far_refs:
        views += [ref.at[0:packet], ref.at[packet : 2 * packet]]
    return views


def pack_kernel(*refs):
    sources, (same_ref, cross_ref) = refs[:7], refs[7:9]
    near, wide_ref, sems = refs[9:16], refs[16], refs[17]
    pos_ref, q_ref, g_ref, k_ref, v_ref, n_ref, d_ref = near
    copies = [
        pltpu.make_async_copy(source, target, sems.at[i])
        for i, (source, target) in enumerate(zip(sources, near))
    ]
    for i in (1, 2, 3, 4, 5, 6, 0):
        copies[i].start()
    rows = q_ref.shape[0]
    tall = pos_ref.shape[0]
    planes = tall // rows
    chips = same_ref.shape[0]
    kv_heads = 2 * chips
    group = q_ref.shape[1] // k_ref.shape[1]
    block = lax.axis_index("ctx")
    odd_core = (block & 1) == 1
    lane = lane_of((rows, LANES))
    low = lane < HEAD_WIDTH
    scale = HEAD_WIDTH ** (-0.5)

    def put(chip, at, first, second):
        to = (block >> 1) ^ chip
        same_ref[to, at : at + rows, :] = jnp.where(odd_core, second, first).astype(BF16)
        cross_ref[to, at : at + rows, :] = jnp.where(odd_core, first, second).astype(BF16)

    def query_tiles(m):
        cols = slice(m * LANES, (m + 1) * LANES)
        q = q_ref[:, cols].astype(F32) * scale
        g = g_ref[:, cols].astype(F32)
        even = jnp.where(low, q, pltpu.roll(g, HEAD_WIDTH, 1))
        odd = jnp.where(low, pltpu.roll(q, HEAD_WIDTH, 1), g)
        return even, odd

    copies[1].wait()
    copies[2].wait()
    pairs = group // 2
    for chip in range(chips):
        for e in range(pairs):
            here = query_tiles(2 * chip * pairs + e)
            there = query_tiles((2 * chip + 1) * pairs + e)
            for side in range(2):
                put(chip, (2 * e + side) * rows, here[side], there[side])
    at = group * rows
    copies[3].wait()
    copies[4].wait()
    for chip in range(chips):
        cols = slice(chip * LANES, (chip + 1) * LANES)
        k = k_ref[:, cols].astype(F32)
        v = v_ref[:, cols].astype(F32)
        even = jnp.where(low, k, pltpu.roll(v, HEAD_WIDTH, 1))
        odd = jnp.where(low, pltpu.roll(k, HEAD_WIDTH, 1), v)
        put(chip, at, even, odd)
    at = at + rows
    copies[5].wait()
    copies[6].wait()
    copies[0].wait()
    wide_ref[...] = jnp.zeros(wide_ref.shape, F32)
    wide_ref[0, 0 : n_ref.shape[0], :] = n_ref[...]
    wide_ref[1, 0 : d_ref.shape[0], :] = d_ref[...]
    tall_lane = lane_of((tall, LANES))
    row_half = tall // 2
    lead = (pos_ref[0] // row_half).astype(F32)
    width = PIECES * 2 * group
    first = planes * width
    tiles = []
    for parity in range(2):
        spread = jnp.zeros((tall, LANES), F32)
        for t in range(2):
            rest = wide_ref[t].T
            for s in range(PIECES):
                piece = rest.astype(BF16).astype(F32)
                rest = rest - piece
                to = s * 2 * group + t * group
                here = (tall_lane >= to) & (tall_lane < to + group)
                moved = pltpu.roll(piece, (to - group * parity) % LANES, 1)
                spread = jnp.where(here, moved, spread)
        tile = jnp.zeros((rows, LANES), F32)
        for h in range(planes):
            part = spread[h * rows : (h + 1) * rows]
            moved = pltpu.roll(part, h * width, 1) if h else part
            tile = jnp.where((lane >= h * width) & (lane < (h + 1) * width), moved, tile)
        tiles.append(tile)
    same = jnp.where(odd_core, tiles[1], tiles[0])
    cross = jnp.where(odd_core, tiles[0], tiles[1])
    in_lead = (lane >= first) & (lane < first + planes * kv_heads)
    for chip in range(chips):
        mine = in_lead & (lane % kv_heads == 2 * chip)
        same_ref[chip, at : at + rows, :] = jnp.where(mine, lead, same).astype(BF16)
        mine = in_lead & (lane % kv_heads == 2 * chip + 1)
        cross_ref[chip, at : at + rows, :] = jnp.where(mine, lead, cross).astype(BF16)


def join_kernel(same_ref, cross_ref, *out_refs):
    packet = same_ref.shape[1]
    for m, ref in enumerate(out_refs):
        ref[0:packet, :] = same_ref[m + 1]
        ref[packet : 2 * packet, :] = cross_ref[m + 1]


def spread_kernel(*refs):
    chips = refs[0].shape[0]
    slots = slots_of(refs[:2], refs[2 : chips + 1])
    send_refs = refs[chips + 1 :]
    blocks = len(slots)
    packet = slots[0].shape[0]
    rows = send_refs[0].shape[0] // (blocks + 1)
    plane = lax.axis_index("head")
    width = LANES // blocks
    lane = lane_of((rows, LANES))
    tiles = [slot[packet - rows : packet, :].astype(F32) for slot in slots]
    for j in range(len(send_refs)):
        wanted = plane ^ j
        tile = jnp.zeros((rows, LANES), F32)
        for b in range(blocks):
            shift = lax.rem(b * width - wanted * width + LANES, LANES)
            here = (lane >= b * width) & (lane < (b + 1) * width)
            tile = jnp.where(here, pltpu.roll(tiles[b], shift, 1), tile)
        ref = send_refs[0 if j == 0 else 1 + ORDER.index(j)]
        for b in range(blocks):
            ref[b * rows : (b + 1) * rows, :] = slots[b][packet - 2 * rows : packet - rows, :]
        ref[blocks * rows : (blocks + 1) * rows, :] = tile.astype(BF16)


def make_attend_others(planes):
    def attend_others_kernel(*refs):
        chips = refs[0].shape[0]
        slots = slots_of(refs[:2], refs[2 : chips + 1])
        own_ref, refs = refs[chips + 1], refs[chips + 2 :]
        got = [refs[ORDER.index(j)] for j in range(1, planes)]
        send_refs = refs[planes - 1 : 2 * planes - 2]
        right_ref, both_ref, scores_ref, query_ref, left_ref, prob_ref = refs[2 * planes - 2 :]
        blocks = len(slots)
        rows = own_ref.shape[0] // (blocks + 1)
        group = slots[0].shape[0] // rows - 2
        tokens = blocks * rows
        width = LANES // blocks
        plane = lax.axis_index("head")
        holder = plane ^ (lax.axis_index("ctx") // (blocks // planes))
        lane = lane_of((rows, LANES))
        lane_row = lane_of((1, LANES))
        first = planes * width

        tile = own_ref[tokens : tokens + rows, :].astype(F32)
        for j in range(1, planes):
            other = got[j - 1][tokens : tokens + rows, :].astype(F32)
            tile = jnp.where(holder == j, other, tile)
        folds = (tile, pltpu.roll(tile, LANES // 2, 1))

        lead = jnp.zeros((1, LANES), F32)
        for b in range(blocks):
            at = (group + 1) * rows
            lead = lead + slots[b][at : at + rows, :].astype(F32)[0:1]
        key_plane = (lane_row - first) // blocks
        per_half = planes // 2
        count = 2 * blocks

        def place(lead_of, which):
            front = per_half * lead_of + which
            back = per_half * (count - 1 - lead_of) + (which - per_half)
            return jnp.where(which < per_half, front, back)

        key_place = place(lead, key_plane.astype(F32))
        in_mask = (lane_row >= first) & (lane_row < first + planes * blocks)

        low = lane < HEAD_WIDTH
        nothing = jnp.zeros((rows, LANES), BF16)
        for e in range(group):
            for b in range(blocks):
                pair = slots[b][e * rows : (e + 1) * rows, :]
                at = b * rows
                both_ref[e * tokens + at : e * tokens + at + rows, :] = pair
                right_ref[e, at : at + rows, 0:LANES] = jnp.where(low, pair, nothing)
                at = tokens + at
                right_ref[e, at : at + rows, 0:LANES] = jnp.where(low, nothing, pair)
        for b in range(blocks):
            lead_b = jnp.sum(
                jnp.where(lane_row == first + b, lead, 0.0), axis=1, keepdims=True
            )
            query_place = place(lead_b, plane.astype(F32))
            hidden = jnp.where(in_mask & (key_place > query_place), MASKED, 0.0)
            fold = folds[(b * width) // (LANES // 2)]
            at = (b * width) % (LANES // 2)
            near = (lane >= at) & (lane < at + width)
            for e in range(group):
                norm = jnp.where(near & (lane % (2 * group) == e), fold, hidden)
                delta = jnp.where(near & (lane % (2 * group) == group + e), fold, 0.0)
                down = slice(b * rows, (b + 1) * rows)
                right_ref[e, down, LANES:] = norm.astype(BF16)
                down = slice(tokens + b * rows, tokens + (b + 1) * rows)
                right_ref[e, down, LANES:] = delta.astype(BF16)

        for j in range(1, planes):
            kv = got[j - 1][0:tokens, :]
            scores_here = scores_ref.at[(j - 1) * tokens : j * tokens]
            kv_sum = pair_sums(
                kv, first + (plane ^ j) * blocks, first, rows, None,
                left_ref, right_ref, both_ref, prob_ref, scores_here,
            )
            send_refs[ORDER.index(j)][...] = kv_sum.astype(BF16)
            query_ref[j - 1] = kv

    return attend_others_kernel


def pair_sums(
    kv, mark_from, first, rows, allowed, left_ref, right_ref, both_ref, prob_ref, score_ref
):
    tokens = kv.shape[0]
    group = right_ref.shape[0]
    key_row = lax.broadcasted_iota(jnp.int32, (tokens, LANES), 0)
    wide_lane = lane_of((tokens, LANES))
    low = wide_lane < HEAD_WIDTH
    mark = mark_from + key_row // rows
    ones = jnp.where((wide_lane < first) | (wide_lane == mark), -1.0, 0.0)
    left_ref[:, 0:LANES] = kv
    left_ref[:, LANES:] = ones.astype(BF16)
    for e in range(group):
        both = lax.dot_general(
            left_ref[...],
            right_ref[e],
            (((1,), (1,)), ((), ())),
            preferred_element_type=F32,
        )
        prob = jnp.exp(both[:, 0:tokens])
        if allowed is not None:
            prob = jnp.where(allowed, prob, 0.0)
        score = prob * both[:, tokens:]
        across = slice(e * tokens, (e + 1) * tokens)
        prob_ref[:, across] = prob.astype(BF16)
        score_ref[:, across] = score.astype(BF16)
    value_side = jnp.dot(prob_ref[...], both_ref[...], preferred_element_type=F32)
    key_side = jnp.dot(score_ref[...], both_ref[...], preferred_element_type=F32)
    return jnp.where(low, key_side, value_side)


def attend_own_kernel(
    own_ref, right_ref, both_ref, scores_ref, keys_ref, out_ref, sum_ref, left_ref, prob_ref, score_ref
):
    others, tokens, _ = keys_ref.shape
    blocks = out_ref.shape[0]
    rows = tokens // blocks
    block = lax.axis_index("ctx")
    group = right_ref.shape[0]
    plane = lax.axis_index("head")
    planes = others + 1
    first = planes * (LANES // blocks)
    square_key = lax.broadcasted_iota(jnp.int32, (tokens, tokens), 0)
    square_query = lane_of((tokens, tokens))
    allowed = (square_key <= square_query) | (square_key // rows != square_query // rows)
    kv = own_ref[0:tokens, :]
    sum_ref[...] = pair_sums(
        kv, first + plane * blocks, first, rows, allowed,
        left_ref, right_ref, both_ref, prob_ref, score_ref,
    )
    turned = kv.astype(F32).T[0:HEAD_WIDTH].astype(BF16)
    query_sum = jnp.dot(turned, score_ref[...], preferred_element_type=F32)
    for j in range(others):
        turned = keys_ref[j].astype(F32).T[0:HEAD_WIDTH].astype(BF16)
        query_sum = query_sum + jnp.dot(
            turned, scores_ref[j * tokens : (j + 1) * tokens, :], preferred_element_type=F32
        )
    scale = HEAD_WIDTH ** (-0.5)
    for m in range(group // 2):
        pair = jnp.concatenate(
            [
                query_sum[:, 2 * m * tokens : (2 * m + 1) * tokens],
                query_sum[:, (2 * m + 1) * tokens : (2 * m + 2) * tokens],
            ],
            0,
        )
        done = (pair.T * scale).astype(BF16)
        for b in range(blocks):
            out_ref[block ^ b, m * rows : (m + 1) * rows, :] = done[b * rows : (b + 1) * rows]


def total_kernel(sum_ref, *refs):
    got, out_ref = refs[:-2], refs[-1]
    total = sum_ref[...]
    for ref in got:
        total = total + ref[...].astype(F32)
    rows = out_ref.shape[1]
    block = lax.axis_index("ctx")
    for b in range(out_ref.shape[0]):
        out_ref[block ^ b] = total[b * rows : (b + 1) * rows].astype(BF16)


def unpack_kernel(in_ref, q_ref, k_ref, v_ref):
    rows = q_ref.shape[0]
    heads = in_ref.shape[0]
    tiles = in_ref.shape[1] // rows - 1
    low = lane_of((rows, LANES)) < HEAD_WIDTH
    for c in range(heads):
        for m in range(tiles):
            at = (c * tiles + m) * LANES
            q_ref[:, at : at + LANES] = in_ref[c, m * rows : (m + 1) * rows, :]
    for m in range(heads // 2):
        even = in_ref[2 * m, tiles * rows : (tiles + 1) * rows, :].astype(F32)
        odd = in_ref[2 * m + 1, tiles * rows : (tiles + 1) * rows, :].astype(F32)
        cols = slice(m * LANES, (m + 1) * LANES)
        k_ref[:, cols] = jnp.where(low, even, pltpu.roll(odd, HEAD_WIDTH, 1)).astype(BF16)
        v_ref[:, cols] = jnp.where(low, pltpu.roll(even, HEAD_WIDTH, 1), odd).astype(BF16)


def whole(shape):
    return pl.BlockSpec(shape, lambda: (0,) * len(shape))


ROOMY = pltpu.CompilerParams(vmem_limit_bytes=24 << 20)
KEPT = pl.BlockSpec(memory_space=pltpu.VMEM)


def kept(*arrays):
    return [pltpu.with_memory_space_constraint(a, pltpu.VMEM) for a in arrays]


def by_heads(
    query_input,
    key_input,
    value_input,
    output_gradient,
    log_softmax_norm,
    output_delta_rows,
    positions,
):
    blocks = lax.axis_size("ctx")
    planes = lax.axis_size("head")
    rows = query_input.shape[0]
    tokens = blocks * rows
    group = query_input.shape[1] // key_input.shape[1]
    packet = (group + 2) * rows
    tall = positions.shape[0]
    norm_cols, delta_cols = log_softmax_norm.T, output_delta_rows.T
    arguments = (
        positions,
        query_input,
        output_gradient,
        key_input,
        value_input,
        norm_cols,
        delta_cols,
    )
    chips = blocks // 2
    half = pltpu.VMEM((chips, packet, LANES), BF16)
    same, cross = pl.pallas_call(
        pack_kernel,
        name="pack",
        compiler_params=ROOMY,
        out_shape=[half, half],
        in_specs=[pl.BlockSpec(memory_space=pl.ANY)] * len(arguments),
        out_specs=[KEPT, KEPT],
        scratch_shapes=[
            pltpu.SMEM(a.shape, a.dtype) if a.ndim == 1 else pltpu.VMEM(a.shape, a.dtype)
            for a in arguments
        ]
        + [pltpu.VMEM((2, LANES, tall), F32), pltpu.SemaphoreType.DMA((len(arguments),))],
    )(*[pltpu.with_memory_space_constraint(a, pltpu.HBM) for a in arguments])

    def trade(array, by):
        return lax.ppermute(array, "ctx", [(i, i ^ by) for i in range(blocks)])

    cross = trade(cross, 1)
    joined = pl.pallas_call(
        join_kernel,
        name="join",
        compiler_params=ROOMY,
        out_shape=[pltpu.VMEM((2 * packet, LANES), BF16)] * (chips - 1),
        in_specs=[KEPT] * 2,
        out_specs=[KEPT] * (chips - 1),
    )(*kept(same, cross))
    joined = [trade(joined[m], 2 * (m + 1)) for m in range(chips - 1)]
    packets = kept(same, cross, *joined)
    own, *sends = pl.pallas_call(
        spread_kernel,
        name="spread",
        compiler_params=ROOMY,
        out_shape=[pltpu.VMEM((tokens + rows, LANES), BF16)] * planes,
        in_specs=[KEPT] * (chips + 1),
        out_specs=[KEPT] * planes,
    )(*packets)

    def swap(array, by):
        return lax.ppermute(array, "head", [(i, i ^ by) for i in range(planes)])

    moved = {j: swap(sends[ORDER.index(j)], j) for j in ORDER}
    got = [moved[j] for j in ORDER]
    wide = group * tokens
    *parts, right, both, scores, keys = pl.pallas_call(
        make_attend_others(planes),
        name="attend_others",
        compiler_params=ROOMY,
        out_shape=[pltpu.VMEM((tokens, LANES), BF16)] * (planes - 1)
        + [
            pltpu.VMEM((group, 2 * tokens, 2 * LANES), BF16),
            pltpu.VMEM((wide, LANES), BF16),
            pltpu.VMEM(((planes - 1) * tokens, wide), BF16),
            pltpu.VMEM((planes - 1, tokens, LANES), BF16),
        ],
        in_specs=[KEPT] * (chips + 1 + planes),
        out_specs=[KEPT] * (planes + 3),
        scratch_shapes=[
            pltpu.VMEM((tokens, 2 * LANES), BF16),
            pltpu.VMEM((tokens, wide), BF16),
        ],
    )(*packets, *kept(own, *got))
    moved = {j: swap(parts[ORDER.index(j)], j) for j in ORDER}
    parts = [moved[j] for j in ORDER]
    packet = (group // 2 + 1) * rows
    back, total = pl.pallas_call(
        attend_own_kernel,
        name="attend_own",
        compiler_params=ROOMY,
        out_shape=[
            jax.ShapeDtypeStruct((blocks, packet, LANES), BF16),
            pltpu.VMEM((tokens, LANES), F32),
        ],
        in_specs=[KEPT] * 5,
        out_specs=[whole((blocks, packet, LANES)), KEPT],
        scratch_shapes=[
            pltpu.VMEM((tokens, 2 * LANES), BF16),
            pltpu.VMEM((tokens, wide), BF16),
            pltpu.VMEM((tokens, wide), BF16),
        ],
        cost_estimate=pl.CostEstimate(
            flops=4 * wide * tokens * LANES * 4, transcendentals=wide * tokens, bytes_accessed=1 << 22
        ),
    )(*kept(own, right, both, scores, keys))
    last = pl.BlockSpec((blocks, rows, LANES), lambda i: (0, group // 2, 0))
    back = pl.pallas_call(
        total_kernel,
        name="total",
        compiler_params=ROOMY,
        grid=(1,),
        out_shape=jax.ShapeDtypeStruct(back.shape, BF16),
        in_specs=[KEPT] * planes + [pl.BlockSpec(memory_space=pl.ANY)],
        out_specs=last,
        input_output_aliases={planes: 0},
    )(*kept(total, *parts), back)
    back = lax.all_to_all(back, "ctx", split_axis=0, concat_axis=0, tiled=True)
    (back,) = kept(back)
    shapes = [query_input.shape, key_input.shape, value_input.shape]
    return tuple(
        pl.pallas_call(
            unpack_kernel,
            name="unpack",
        compiler_params=ROOMY,
            out_shape=[jax.ShapeDtypeStruct(s, BF16) for s in shapes],
            in_specs=[KEPT],
            out_specs=[whole(s) for s in shapes],
        )(back)
    )


def solution(mesh):
    def on_each(*args):
        query_input, key_input = args[0], args[1]
        kv_heads = key_input.shape[1] // HEAD_WIDTH
        group = query_input.shape[1] // key_input.shape[1]
        blocks, planes = mesh.shape["ctx"], mesh.shape["head"]
        by_head = (
            blocks == kv_heads
            and group == 4
            and planes == 4
            and kv_heads == 8
            and query_input.shape[0] % 16 == 0
        )
        return (by_heads if by_head else on_device)(*args)

    return jax.shard_map(
        on_each,
        mesh=mesh,
        in_specs=(
            P(("ctx", "head"), None),
            P(("ctx", "head"), None),
            P(("ctx", "head"), None),
            P(("ctx", "head"), None),
            P("ctx", "head"),
            P("ctx", "head"),
            P("ctx"),
        ),
        out_specs=(P(("ctx", "head"), None), P(("ctx", "head"), None), P(("ctx", "head"), None)),
        check_vma=False,
    )
```

```python
import jax
import jax.numpy as jnp
from jax import lax
from jax.experimental import pallas as pl
from jax.experimental.pallas import tpu as pltpu
from jax.sharding import PartitionSpec as P

HEAD_WIDTH = 64
LANES = 128
PIECES = 2
NOTE_ROWS = 8
CHIP_ORDER = (1, 2, 3)
MASKED = 16384.0
F32 = jnp.float32
BF16 = jnp.bfloat16


def for_sending(array):
    return jax.tree.map(lambda a: a.astype(jnp.bfloat16) if a.dtype == jnp.float32 else a, array)


def from_behind(array, axis, by):
    count = lax.axis_size(axis)
    return lax.ppermute(array, axis, [(i, (i + by) % count) for i in range(count)])


def block_terms(
    query, grad_rows, norm_rows, delta_part, query_pos, key_block, value_block, key_pos
):
    row_count = query.shape[0]
    col_count = key_block.shape[0]
    kv_heads = key_block.shape[1] // HEAD_WIDTH
    query_group_width = query.shape[1] // (kv_heads * HEAD_WIDTH)
    score_scale = HEAD_WIDTH ** (-0.5)
    query_per_head = query.reshape(row_count, kv_heads, query_group_width, HEAD_WIDTH)
    gradient_per_head = grad_rows.reshape(row_count, kv_heads, query_group_width, HEAD_WIDTH)
    key_per_head = key_block.reshape(col_count, kv_heads, HEAD_WIDTH)
    value_per_head = value_block.reshape(col_count, kv_heads, HEAD_WIDTH)
    scores = (
        jnp.einsum(
            "qhgd,khd->qhgk", query_per_head, key_per_head, preferred_element_type=jnp.float32
        )
        * score_scale
    )
    visible = (query_pos[:, None] >= key_pos[None, :])[:, None, None, :]
    norm_cols = norm_rows.reshape(row_count, kv_heads, query_group_width, 1)
    probabilities = jnp.where(visible, jnp.exp(scores - norm_cols), 0.0)
    grad_prob = jnp.einsum(
        "qhgd,khd->qhgk", gradient_per_head, value_per_head, preferred_element_type=jnp.float32
    )
    grad_score = probabilities * (
        grad_prob - delta_part.reshape(row_count, kv_heads, query_group_width, 1)
    )
    prob_rounded = probabilities.astype(jnp.bfloat16)
    score_rounded = grad_score.astype(jnp.bfloat16)
    value_term = jnp.einsum(
        "qhgk,qhgd->khd", prob_rounded, gradient_per_head, preferred_element_type=jnp.float32
    )
    key_term = score_scale * jnp.einsum(
        "qhgk,qhgd->khd", score_rounded, query_per_head, preferred_element_type=jnp.float32
    )
    query_term = score_scale * jnp.einsum(
        "qhgk,khd->qhgd", score_rounded, key_per_head, preferred_element_type=jnp.float32
    )
    return (
        query_term.reshape(row_count, -1),
        key_term.reshape(col_count, -1),
        value_term.reshape(col_count, -1),
    )


def no_terms(operands):
    query = operands[0]
    key_block = operands[5]
    return (
        jnp.zeros(query.shape, jnp.float32),
        jnp.zeros(key_block.shape, jnp.float32),
        jnp.zeros(key_block.shape, jnp.float32),
    )


def all_terms(operands):
    return block_terms(*operands)


def pair_terms(query, grad_rows, norm_rows, delta_part, query_pos, key_block, value_block, key_pos):
    row_half = query.shape[0] // 2
    col_half = key_block.shape[0] // 2
    zero_cols = jnp.zeros((col_half, key_block.shape[1]), jnp.float32)
    key_sums = [zero_cols, zero_cols]
    value_sums = [zero_cols, zero_cols]
    query_parts = []
    for row_side in range(2):
        rows_here = slice(row_side * row_half, (row_side + 1) * row_half)
        query_sum = jnp.zeros((row_half, query.shape[1]), jnp.float32)
        for col_side in range(2):
            cols_here = slice(col_side * col_half, (col_side + 1) * col_half)
            operands = (
                query[rows_here],
                grad_rows[rows_here],
                norm_rows[rows_here],
                delta_part[rows_here],
                query_pos[rows_here],
                key_block[cols_here],
                value_block[cols_here],
                key_pos[cols_here],
            )
            reached = jnp.any(query_pos[rows_here][:, None] >= key_pos[cols_here][None, :])
            query_term, key_term, value_term = lax.cond(reached, all_terms, no_terms, operands)
            query_sum = query_sum + query_term
            key_sums[col_side] = key_sums[col_side] + key_term
            value_sums[col_side] = value_sums[col_side] + value_term
        query_parts.append(query_sum)
    return (
        jnp.concatenate(query_parts, 0),
        jnp.concatenate(key_sums, 0),
        jnp.concatenate(value_sums, 0),
    )


def pass_keys(traveler, offset):
    return from_behind((for_sending(traveler[0]), for_sending(traveler[1])), "ctx", offset)


def pass_sums(traveler, offset):
    return from_behind((traveler[2], traveler[3], traveler[4]), "ctx", offset)


def on_device(
    query_input,
    key_input,
    value_input,
    output_gradient,
    log_softmax_norm,
    output_delta_rows,
    positions,
):
    query, key_local, value_local, grad_rows = (
        lax.all_to_all(query_input, "head", split_axis=1, concat_axis=0, tiled=True),
        lax.all_to_all(key_input, "head", split_axis=1, concat_axis=0, tiled=True),
        lax.all_to_all(value_input, "head", split_axis=1, concat_axis=0, tiled=True),
        lax.all_to_all(output_gradient, "head", split_axis=1, concat_axis=0, tiled=True),
    )
    query_pos = positions.astype(jnp.float32)
    row_count = query.shape[0]
    feature_width = key_local.shape[1]
    grad_query = jnp.zeros(query.shape, jnp.float32)

    def visit(key_block, value_block, key_pos):
        return pair_terms(
            query,
            grad_rows,
            log_softmax_norm,
            output_delta_rows,
            query_pos,
            key_block,
            value_block,
            key_pos,
        )

    offsets = (1,)
    bounds = ((0, row_count),)
    travelers = tuple(
        (
            (
                key_local,
                value_local,
                jnp.zeros((upper_row - lower_row, feature_width), jnp.float32),
                jnp.zeros((upper_row - lower_row, feature_width), jnp.float32),
                query_pos,
            )
            for lower_row, upper_row in bounds
        )
    )

    def absorb_all(query_sum, travelers):
        updated = []
        for traveler in travelers:
            key_block, value_block, key_acc, value_acc, key_pos = traveler
            query_term, key_term, value_term = visit(key_block, value_block, key_pos)
            query_sum = query_sum + query_term
            updated.append(
                (key_block, value_block, key_acc + key_term, value_acc + value_term, key_pos)
            )
        return (query_sum, tuple(updated))

    def cycle_turn(turn_index, running):
        query_sum, travelers = absorb_all(running[0], running[1])
        moved = []
        for traveler, offset in zip(travelers, offsets):
            key_block, value_block = pass_keys(traveler, offset)
            key_acc, value_acc, key_pos = pass_sums(traveler, offset)
            moved.append((key_block, value_block, key_acc, value_acc, key_pos))
        return (query_sum, tuple(moved))

    grad_query, travelers = lax.fori_loop(
        0, lax.axis_size("ctx") - 1, cycle_turn, (grad_query, travelers)
    )
    grad_query, travelers = absorb_all(grad_query, travelers)
    returned = [pass_sums(traveler, offset) for traveler, offset in zip(travelers, offsets)]
    key_gradient = jnp.concatenate([arrived[0] for arrived in returned], 0)
    value_gradient = jnp.concatenate([arrived[1] for arrived in returned], 0)
    query_out, key_out, value_out = (
        lax.all_to_all(
            grad_query.astype(jnp.bfloat16), "head", split_axis=0, concat_axis=1, tiled=True
        ),
        lax.all_to_all(
            key_gradient.astype(jnp.bfloat16), "head", split_axis=0, concat_axis=1, tiled=True
        ),
        lax.all_to_all(
            value_gradient.astype(jnp.bfloat16), "head", split_axis=0, concat_axis=1, tiled=True
        ),
    )
    return (query_out, key_out, value_out)


def lane_of(shape):
    return lax.broadcasted_iota(jnp.int32, shape, len(shape) - 1)


def pair_sums(kv, mark_from, first, rows, allowed, left_ref, right_ref, prob_ref, score_ref):
    tokens = kv.shape[0]
    group = right_ref.shape[0]
    key_row = lax.broadcasted_iota(jnp.int32, (tokens, LANES), 0)
    wide_lane = lane_of((tokens, LANES))
    low = wide_lane < HEAD_WIDTH
    mark = mark_from + key_row // rows
    ones = jnp.where((wide_lane < first) | (wide_lane == mark), -1.0, 0.0)
    left_ref[:, 0:LANES] = kv
    left_ref[:, LANES:] = ones.astype(BF16)
    for e in range(group):
        both = lax.dot_general(
            left_ref[...],
            right_ref[e, 0 : 2 * tokens],
            (((1,), (1,)), ((), ())),
            preferred_element_type=F32,
        )
        prob = jnp.exp(both[:, 0:tokens])
        if allowed is not None:
            prob = jnp.where(allowed, prob, 0.0)
        score = prob * both[:, tokens:]
        across = slice(e * tokens, (e + 1) * tokens)
        prob_ref[:, across] = prob.astype(BF16)
        score_ref[:, across] = score.astype(BF16)
    pairs = jnp.concatenate(
        [right_ref[e, 2 * tokens : 3 * tokens, 0:LANES] for e in range(group)], 0
    )
    value_side = jnp.dot(prob_ref[...], pairs, preferred_element_type=F32)
    key_side = jnp.dot(score_ref[...], pairs, preferred_element_type=F32)
    return jnp.where(low, key_side, value_side)


def pack_kernel(*refs):
    sources, (out_ref, same_ref, cross_ref) = refs[:7], refs[7:10]
    near, key_ref, sems = refs[10:17], refs[17], refs[18]
    pos_ref, q_ref, g_ref, k_ref, v_ref, n_ref, d_ref = near
    copies = [
        pltpu.make_async_copy(source, target, sems.at[i])
        for i, (source, target) in enumerate(zip(sources, near))
    ]
    for i in (5, 6, 0, 3, 4, 1, 2):
        copies[i].start()
    rows = q_ref.shape[0]
    tall = pos_ref.shape[0]
    planes = tall // rows
    chips = same_ref.shape[0]
    group = q_ref.shape[1] // k_ref.shape[1]
    block = lax.axis_index("ctx")
    odd_core = (block & 1) == 1
    lane = lane_of((rows, LANES))
    low = lane < HEAD_WIDTH
    scale = HEAD_WIDTH ** (-0.5)

    copies[5].wait()
    copies[6].wait()
    copies[0].wait()
    lead = (pos_ref[0] // (tall // 2)).astype(F32)
    eight = NOTE_ROWS
    sub = lax.broadcasted_iota(jnp.int32, (eight, LANES), 0)
    quarter = lane_of((eight, LANES)) // rows
    turns = []
    for s in range(PIECES):
        for t, ref in enumerate((n_ref, d_ref)):
            rest = ref[...]
            for _ in range(s):
                rest = rest - rest.astype(BF16).astype(F32)
            piece = rest.astype(BF16).astype(F32)
            turns.append([pltpu.roll(piece, d * rows, 1) if d else piece for d in range(planes)])
    for parity in range(2):
        for h in range(planes):
            note = jnp.where(sub == len(turns), lead, 0.0)
            for r, turn in enumerate(turns):
                for e in range(group):
                    head = group * parity + e
                    line = turn[(e - h) % planes][head : head + 1, :]
                    note = jnp.where((sub == r) & (quarter == e), line, note)
            note = note.astype(BF16)
            for c in range(parity, 2 * chips, 2):
                key_ref[c * planes + h, rows : rows + eight, :] = note

    copies[3].wait()
    copies[4].wait()
    for chip in range(chips):
        cols = slice(chip * LANES, (chip + 1) * LANES)
        k = k_ref[:, cols].astype(F32)
        v = v_ref[:, cols].astype(F32)
        even = jnp.where(low, k, pltpu.roll(v, HEAD_WIDTH, 1)).astype(BF16)
        odd = jnp.where(low, pltpu.roll(k, HEAD_WIDTH, 1), v).astype(BF16)
        for h in range(planes):
            key_ref[2 * chip * planes + h, 0:rows, :] = even
            key_ref[(2 * chip + 1) * planes + h, 0:rows, :] = odd

    out = pltpu.make_async_copy(key_ref, out_ref, sems.at[7])
    out.start()

    def query_tiles(m):
        cols = slice(m * LANES, (m + 1) * LANES)
        q = q_ref[:, cols].astype(F32) * scale
        g = g_ref[:, cols].astype(F32)
        even = jnp.where(low, q, pltpu.roll(g, HEAD_WIDTH, 1))
        odd = jnp.where(low, pltpu.roll(q, HEAD_WIDTH, 1), g)
        return even, odd

    copies[1].wait()
    copies[2].wait()
    pairs = group // 2
    for chip in range(chips):
        to = (block >> 1) ^ chip
        for e in range(pairs):
            here = query_tiles(2 * chip * pairs + e)
            there = query_tiles((2 * chip + 1) * pairs + e)
            for side in range(2):
                first, second = here[side], there[side]
                at = (2 * e + side) * rows
                same = jnp.where(odd_core, second, first).astype(BF16)
                cross = jnp.where(odd_core, first, second).astype(BF16)
                same_ref[to, at : at + rows, :] = same
                cross_ref[to, at : at + rows, :] = cross
    out.wait()


def join_kernel(same_ref, cross_ref, *out_refs):
    packet = same_ref.shape[1]
    for m, ref in enumerate(out_refs):
        ref[0:packet, :] = same_ref[CHIP_ORDER[m]]
        ref[packet : 2 * packet, :] = cross_ref[CHIP_ORDER[m]]


def prepare_kernel(same_ref, cross_ref, *refs):
    far_refs, right_ref = refs[:-1], refs[-1]
    packet = same_ref.shape[1]
    group = right_ref.shape[0]
    tokens = right_ref.shape[1] // 3
    rows = packet // group
    block = lax.axis_index("ctx")
    slots = {0: same_ref.at[0], 1: cross_ref.at[0]}
    for m, ref in enumerate(far_refs):
        slots[2 * CHIP_ORDER[m]] = ref.at[0:packet]
        slots[2 * CHIP_ORDER[m] + 1] = ref.at[packet : 2 * packet]
    low = lane_of((rows, LANES)) < HEAD_WIDTH
    nothing = jnp.zeros((rows, LANES), BF16)
    for i, slot in slots.items():
        at = pl.multiple_of((block ^ i) * rows, rows)
        for e in range(group):
            pair = slot[e * rows : (e + 1) * rows, :]
            right_ref[e, pl.ds(2 * tokens + at, rows), 0:LANES] = pair
            right_ref[e, pl.ds(at, rows), 0:LANES] = jnp.where(low, pair, nothing)
            right_ref[e, pl.ds(tokens + at, rows), 0:LANES] = jnp.where(low, nothing, pair)


def plane_keys(key_ref, which, blocks, rows):
    planes = key_ref.shape[0] // blocks
    return jnp.concatenate([key_ref[b * planes + which, 0:rows, :] for b in range(blocks)], 0)


def attend_kernel(
    ready_ref, key_ref, right_ref, out_ref, same_ref, cross_ref,
    scores_ref, wide_ref, left_ref, prob_ref, part_ref, all_ref, sems,
):
    group = right_ref.shape[0]
    tokens = right_ref.shape[1] // 3
    blocks, planes, rows, _ = out_ref.shape
    eight = NOTE_ROWS
    count = 2 * PIECES
    plane = lax.axis_index("head")
    holder = lax.axis_index("ctx") // (blocks // planes)
    first = LANES // 2
    lane = lane_of((rows, LANES))
    lane_row = lane_of((1, LANES))
    quarter = lane_of((eight, LANES)) // rows

    lead = jnp.zeros((1, LANES), F32)
    notes = []
    for b in range(blocks):
        note = key_ref[b * planes + holder, rows : rows + eight, :].astype(F32)
        lead = jnp.where(lane_row % blocks == b, note[count : count + 1], lead)
        notes.append(note)
    wide_ref[...] = jnp.zeros(wide_ref.shape, F32)
    per_tile = LANES // rows
    for e in range(group):
        for b in range(blocks):
            spot = b % per_tile
            turn = ((spot - e) * rows) % LANES
            moved = pltpu.roll(notes[b], turn, 1) if turn else notes[b]
            down = slice((b // per_tile) * LANES + e * eight, (b // per_tile) * LANES + (e + 1) * eight)
            wide_ref[down, :] = jnp.where(quarter == spot, moved, wide_ref[down, :])
    columns = [
        wide_ref[m * LANES : (m + 1) * LANES, :].T for m in range(tokens // LANES)
    ]

    key_plane = (lane_row - first) // blocks
    per_half = planes // 2

    def place(lead_of, which):
        front = per_half * lead_of + which
        back = per_half * (2 * blocks - 1 - lead_of) + (which - per_half)
        return jnp.where(which < per_half, front, back)

    key_place = place(lead, key_plane.astype(F32))
    in_mask = (lane_row >= first) & (lane_row < first + planes * blocks)
    for b in range(blocks):
        lead_b = jnp.sum(jnp.where(lane_row == first + b, lead, 0.0), axis=1, keepdims=True)
        query_place = place(lead_b, plane.astype(F32))
        hidden = jnp.where(in_mask & (key_place > query_place), MASKED, 0.0)
        at = (b % per_tile) * rows
        column = columns[b // per_tile][at : at + rows]
        for e in range(group):
            mine = (lane >= e * eight) & (lane < e * eight + count)
            norm = jnp.where(mine & (lane % 2 == 0), column, hidden)
            delta = jnp.where(mine & (lane % 2 == 1), column, 0.0)
            right_ref[e, b * rows : (b + 1) * rows, LANES:] = norm.astype(BF16)
            down = slice(tokens + b * rows, tokens + (b + 1) * rows)
            right_ref[e, down, LANES:] = delta.astype(BF16)

    square_key = lax.broadcasted_iota(jnp.int32, (tokens, tokens), 0)
    square_query = lane_of((tokens, tokens))
    allowed = (square_key <= square_query) | (square_key // rows != square_query // rows)
    copies = []
    for j in range(planes):
        which = plane ^ j
        kv_sum = pair_sums(
            plane_keys(key_ref, which, blocks, rows),
            first + which * blocks, first, rows, None if j else allowed,
            left_ref, right_ref, prob_ref,
            scores_ref.at[j * tokens : (j + 1) * tokens],
        )
        part_ref[j] = kv_sum.astype(BF16).reshape(blocks, rows, LANES)
        copies.append(pltpu.make_async_copy(part_ref.at[j], out_ref.at[:, which], sems.at[j]))
        copies[j].start()
    query_sum = jnp.zeros((HEAD_WIDTH, group * tokens), F32)
    for j in range(planes):
        keys = plane_keys(key_ref, plane ^ j, blocks, rows)
        turned = keys.astype(F32).T[0:HEAD_WIDTH].astype(BF16)
        here = scores_ref[j * tokens : (j + 1) * tokens, :]
        query_sum = query_sum + jnp.dot(turned, here, preferred_element_type=F32)
    scale = HEAD_WIDTH ** (-0.5)
    for m in range(group // 2):
        pair = jnp.concatenate(
            [
                query_sum[:, 2 * m * tokens : (2 * m + 1) * tokens],
                query_sum[:, (2 * m + 1) * tokens : (2 * m + 2) * tokens],
            ],
            0,
        )
        done = (pair.T * scale).astype(BF16)
        all_ref[:, m * rows : (m + 1) * rows, :] = done.reshape(blocks, rows, LANES)
    block = lax.axis_index("ctx")
    for m in range(blocks // 2):
        same_ref[m] = all_ref[block ^ (2 * m)]
        cross_ref[m] = all_ref[block ^ (2 * m + 1)]
    for copy in copies:
        copy.wait()


def unpack_kernel(part_ref, same_ref, cross_ref, *refs):
    chips = same_ref.shape[0]
    far_refs, (q_ref, k_ref, v_ref, all_ref) = refs[: chips - 1], refs[chips - 1 :]
    rows = q_ref.shape[0]
    tall = same_ref.shape[1]
    tiles = tall // rows
    planes = part_ref.shape[0] // (2 * chips)
    block = lax.axis_index("ctx")
    all_ref[block] = same_ref[0]
    all_ref[block ^ 1] = cross_ref[0]
    for m, ref in enumerate(far_refs):
        chip = 2 * CHIP_ORDER[m]
        all_ref[block ^ chip] = ref[0:tall, :]
        all_ref[block ^ (chip + 1)] = ref[tall : 2 * tall, :]
    for c in range(2 * chips):
        for m in range(tiles):
            at = (c * tiles + m) * LANES
            q_ref[:, at : at + LANES] = all_ref[c, m * rows : (m + 1) * rows, :]

    def added(c):
        total = part_ref[c * planes].astype(F32)
        for h in range(1, planes):
            total = total + part_ref[c * planes + h].astype(F32)
        return total

    low = lane_of((rows, LANES)) < HEAD_WIDTH
    for m in range(chips):
        even, odd = added(2 * m), added(2 * m + 1)
        cols = slice(m * LANES, (m + 1) * LANES)
        k_ref[:, cols] = jnp.where(low, even, pltpu.roll(odd, HEAD_WIDTH, 1)).astype(BF16)
        v_ref[:, cols] = jnp.where(low, pltpu.roll(even, HEAD_WIDTH, 1), odd).astype(BF16)


def whole(shape):
    return pl.BlockSpec(shape, lambda: (0,) * len(shape))


ROOMY = pltpu.CompilerParams(vmem_limit_bytes=24 << 20)
KEPT = pl.BlockSpec(memory_space=pltpu.VMEM)


def kept(*arrays):
    return [pltpu.with_memory_space_constraint(a, pltpu.VMEM) for a in arrays]


def by_heads(
    query_input,
    key_input,
    value_input,
    output_gradient,
    log_softmax_norm,
    output_delta_rows,
    positions,
):
    blocks = lax.axis_size("ctx")
    planes = lax.axis_size("head")
    rows = query_input.shape[0]
    tokens = blocks * rows
    group = query_input.shape[1] // key_input.shape[1]
    packet = group * rows
    chips = blocks // 2
    devices = blocks * planes
    wide = group * tokens
    arguments = (
        positions,
        query_input,
        output_gradient,
        key_input,
        value_input,
        log_softmax_norm.T,
        output_delta_rows.T,
    )
    half = pltpu.VMEM((chips, packet, LANES), BF16)
    keys, same, cross = pl.pallas_call(
        pack_kernel,
        name="pack",
        compiler_params=ROOMY,
        out_shape=[jax.ShapeDtypeStruct((devices, rows + NOTE_ROWS, LANES), BF16), half, half],
        in_specs=[pl.BlockSpec(memory_space=pl.ANY)] * len(arguments),
        out_specs=[pl.BlockSpec(memory_space=pl.ANY), KEPT, KEPT],
        scratch_shapes=[
            pltpu.SMEM(a.shape, a.dtype) if a.ndim == 1 else pltpu.VMEM(a.shape, a.dtype)
            for a in arguments
        ]
        + [
            pltpu.VMEM((devices, rows + NOTE_ROWS, LANES), BF16),
            pltpu.SemaphoreType.DMA((len(arguments) + 1,)),
        ],
    )(*[pltpu.with_memory_space_constraint(a, pltpu.HBM) for a in arguments])

    def trade(array, by):
        return lax.ppermute(array, "ctx", [(i, i ^ by) for i in range(blocks)])

    def to_all(array):
        return lax.all_to_all(array, ("ctx", "head"), split_axis=0, concat_axis=0, tiled=True)

    keys = to_all(keys)

    def exchange(same, cross):
        tall = same.shape[1]
        cross = trade(cross, 1)
        joined = pl.pallas_call(
            join_kernel,
            name="join",
            compiler_params=ROOMY,
            out_shape=[pltpu.VMEM((2 * tall, LANES), BF16)] * (chips - 1),
            in_specs=[KEPT] * 2,
            out_specs=[KEPT] * (chips - 1),
        )(*kept(same, cross))
        joined = [trade(array, 2 * CHIP_ORDER[m]) for m, array in enumerate(joined)]
        return kept(same, cross, *joined)

    received = exchange(same, cross)
    right_shape = pltpu.VMEM((group, 3 * tokens, 2 * LANES), BF16)
    right = pl.pallas_call(
        prepare_kernel,
        name="prepare",
        compiler_params=ROOMY,
        out_shape=right_shape,
        in_specs=[KEPT] * (chips + 1),
        out_specs=KEPT,
    )(*received)
    (keys,) = kept(keys)
    tall = group // 2 * rows
    half = pltpu.VMEM((chips, tall, LANES), BF16)
    right, parts, same, cross = pl.pallas_call(
        attend_kernel,
        name="attend",
        compiler_params=ROOMY,
        out_shape=[
            right_shape,
            jax.ShapeDtypeStruct((blocks, planes, rows, LANES), BF16),
            half,
            half,
        ],
        in_specs=[KEPT] * 2,
        out_specs=[KEPT, pl.BlockSpec(memory_space=pl.ANY), KEPT, KEPT],
        input_output_aliases={0: 0},
        scratch_shapes=[
            pltpu.VMEM((planes * tokens, wide), BF16),
            pltpu.VMEM((tokens // LANES * LANES, LANES), F32),
            pltpu.VMEM((tokens, 2 * LANES), BF16),
            pltpu.VMEM((tokens, wide), BF16),
            pltpu.VMEM((planes, blocks, rows, LANES), BF16),
            pltpu.VMEM((blocks, tall, LANES), BF16),
            pltpu.SemaphoreType.DMA((planes,)),
        ],
    )(*kept(right), keys)
    parts = to_all(parts.reshape(devices, rows, LANES))
    received = exchange(same, cross)
    shapes = [query_input.shape, key_input.shape, value_input.shape]
    return tuple(
        pl.pallas_call(
            unpack_kernel,
            name="unpack",
            compiler_params=ROOMY,
            out_shape=[jax.ShapeDtypeStruct(s, BF16) for s in shapes],
            in_specs=[KEPT] * (chips + 2),
            out_specs=[whole(s) for s in shapes],
            scratch_shapes=[pltpu.VMEM((blocks, tall, LANES), BF16)],
        )(*kept(parts), *received)
    )


def solution(mesh):
    def on_each(*args):
        query_input, key_input = args[0], args[1]
        kv_heads = key_input.shape[1] // HEAD_WIDTH
        group = query_input.shape[1] // key_input.shape[1]
        blocks, planes = mesh.shape["ctx"], mesh.shape["head"]
        by_head = (
            blocks == kv_heads
            and group == 4
            and planes == 4
            and kv_heads == 8
            and query_input.shape[0] % 16 == 0
        )
        return (by_heads if by_head else on_device)(*args)

    return jax.shard_map(
        on_each,
        mesh=mesh,
        in_specs=(
            P(("ctx", "head"), None),
            P(("ctx", "head"), None),
            P(("ctx", "head"), None),
            P(("ctx", "head"), None),
            P("ctx", "head"),
            P("ctx", "head"),
            P("ctx"),
        ),
        out_specs=(P(("ctx", "head"), None), P(("ctx", "head"), None), P(("ctx", "head"), None)),
        check_vma=False,
    )
```

```python
import jax
import jax.numpy as jnp
from jax import lax
from jax.experimental import pallas as pl
from jax.experimental.pallas import tpu as pltpu
from jax.sharding import PartitionSpec as P

HEAD_WIDTH = 64
LANES = 128
PIECES = 2
NOTE_ROWS = 8
TOGETHER = 2
CHIP_ORDER = (1, 2, 3)
MASKED = 16384.0
F32 = jnp.float32
BF16 = jnp.bfloat16


def for_sending(array):
    return jax.tree.map(lambda a: a.astype(jnp.bfloat16) if a.dtype == jnp.float32 else a, array)


def from_behind(array, axis, by):
    count = lax.axis_size(axis)
    return lax.ppermute(array, axis, [(i, (i + by) % count) for i in range(count)])


def block_terms(
    query, grad_rows, norm_rows, delta_part, query_pos, key_block, value_block, key_pos
):
    row_count = query.shape[0]
    col_count = key_block.shape[0]
    kv_heads = key_block.shape[1] // HEAD_WIDTH
    query_group_width = query.shape[1] // (kv_heads * HEAD_WIDTH)
    score_scale = HEAD_WIDTH ** (-0.5)
    query_per_head = query.reshape(row_count, kv_heads, query_group_width, HEAD_WIDTH)
    gradient_per_head = grad_rows.reshape(row_count, kv_heads, query_group_width, HEAD_WIDTH)
    key_per_head = key_block.reshape(col_count, kv_heads, HEAD_WIDTH)
    value_per_head = value_block.reshape(col_count, kv_heads, HEAD_WIDTH)
    scores = (
        jnp.einsum(
            "qhgd,khd->qhgk", query_per_head, key_per_head, preferred_element_type=jnp.float32
        )
        * score_scale
    )
    visible = (query_pos[:, None] >= key_pos[None, :])[:, None, None, :]
    norm_cols = norm_rows.reshape(row_count, kv_heads, query_group_width, 1)
    probabilities = jnp.where(visible, jnp.exp(scores - norm_cols), 0.0)
    grad_prob = jnp.einsum(
        "qhgd,khd->qhgk", gradient_per_head, value_per_head, preferred_element_type=jnp.float32
    )
    grad_score = probabilities * (
        grad_prob - delta_part.reshape(row_count, kv_heads, query_group_width, 1)
    )
    prob_rounded = probabilities.astype(jnp.bfloat16)
    score_rounded = grad_score.astype(jnp.bfloat16)
    value_term = jnp.einsum(
        "qhgk,qhgd->khd", prob_rounded, gradient_per_head, preferred_element_type=jnp.float32
    )
    key_term = score_scale * jnp.einsum(
        "qhgk,qhgd->khd", score_rounded, query_per_head, preferred_element_type=jnp.float32
    )
    query_term = score_scale * jnp.einsum(
        "qhgk,khd->qhgd", score_rounded, key_per_head, preferred_element_type=jnp.float32
    )
    return (
        query_term.reshape(row_count, -1),
        key_term.reshape(col_count, -1),
        value_term.reshape(col_count, -1),
    )


def no_terms(operands):
    query = operands[0]
    key_block = operands[5]
    return (
        jnp.zeros(query.shape, jnp.float32),
        jnp.zeros(key_block.shape, jnp.float32),
        jnp.zeros(key_block.shape, jnp.float32),
    )


def all_terms(operands):
    return block_terms(*operands)


def pair_terms(query, grad_rows, norm_rows, delta_part, query_pos, key_block, value_block, key_pos):
    row_half = query.shape[0] // 2
    col_half = key_block.shape[0] // 2
    zero_cols = jnp.zeros((col_half, key_block.shape[1]), jnp.float32)
    key_sums = [zero_cols, zero_cols]
    value_sums = [zero_cols, zero_cols]
    query_parts = []
    for row_side in range(2):
        rows_here = slice(row_side * row_half, (row_side + 1) * row_half)
        query_sum = jnp.zeros((row_half, query.shape[1]), jnp.float32)
        for col_side in range(2):
            cols_here = slice(col_side * col_half, (col_side + 1) * col_half)
            operands = (
                query[rows_here],
                grad_rows[rows_here],
                norm_rows[rows_here],
                delta_part[rows_here],
                query_pos[rows_here],
                key_block[cols_here],
                value_block[cols_here],
                key_pos[cols_here],
            )
            reached = jnp.any(query_pos[rows_here][:, None] >= key_pos[cols_here][None, :])
            query_term, key_term, value_term = lax.cond(reached, all_terms, no_terms, operands)
            query_sum = query_sum + query_term
            key_sums[col_side] = key_sums[col_side] + key_term
            value_sums[col_side] = value_sums[col_side] + value_term
        query_parts.append(query_sum)
    return (
        jnp.concatenate(query_parts, 0),
        jnp.concatenate(key_sums, 0),
        jnp.concatenate(value_sums, 0),
    )


def pass_keys(traveler, offset):
    return from_behind((for_sending(traveler[0]), for_sending(traveler[1])), "ctx", offset)


def pass_sums(traveler, offset):
    return from_behind((traveler[2], traveler[3], traveler[4]), "ctx", offset)


def on_device(
    query_input,
    key_input,
    value_input,
    output_gradient,
    log_softmax_norm,
    output_delta_rows,
    positions,
):
    query, key_local, value_local, grad_rows = (
        lax.all_to_all(query_input, "head", split_axis=1, concat_axis=0, tiled=True),
        lax.all_to_all(key_input, "head", split_axis=1, concat_axis=0, tiled=True),
        lax.all_to_all(value_input, "head", split_axis=1, concat_axis=0, tiled=True),
        lax.all_to_all(output_gradient, "head", split_axis=1, concat_axis=0, tiled=True),
    )
    query_pos = positions.astype(jnp.float32)
    row_count = query.shape[0]
    feature_width = key_local.shape[1]
    grad_query = jnp.zeros(query.shape, jnp.float32)

    def visit(key_block, value_block, key_pos):
        return pair_terms(
            query,
            grad_rows,
            log_softmax_norm,
            output_delta_rows,
            query_pos,
            key_block,
            value_block,
            key_pos,
        )

    offsets = (1,)
    bounds = ((0, row_count),)
    travelers = tuple(
        (
            (
                key_local,
                value_local,
                jnp.zeros((upper_row - lower_row, feature_width), jnp.float32),
                jnp.zeros((upper_row - lower_row, feature_width), jnp.float32),
                query_pos,
            )
            for lower_row, upper_row in bounds
        )
    )

    def absorb_all(query_sum, travelers):
        updated = []
        for traveler in travelers:
            key_block, value_block, key_acc, value_acc, key_pos = traveler
            query_term, key_term, value_term = visit(key_block, value_block, key_pos)
            query_sum = query_sum + query_term
            updated.append(
                (key_block, value_block, key_acc + key_term, value_acc + value_term, key_pos)
            )
        return (query_sum, tuple(updated))

    def cycle_turn(turn_index, running):
        query_sum, travelers = absorb_all(running[0], running[1])
        moved = []
        for traveler, offset in zip(travelers, offsets):
            key_block, value_block = pass_keys(traveler, offset)
            key_acc, value_acc, key_pos = pass_sums(traveler, offset)
            moved.append((key_block, value_block, key_acc, value_acc, key_pos))
        return (query_sum, tuple(moved))

    grad_query, travelers = lax.fori_loop(
        0, lax.axis_size("ctx") - 1, cycle_turn, (grad_query, travelers)
    )
    grad_query, travelers = absorb_all(grad_query, travelers)
    returned = [pass_sums(traveler, offset) for traveler, offset in zip(travelers, offsets)]
    key_gradient = jnp.concatenate([arrived[0] for arrived in returned], 0)
    value_gradient = jnp.concatenate([arrived[1] for arrived in returned], 0)
    query_out, key_out, value_out = (
        lax.all_to_all(
            grad_query.astype(jnp.bfloat16), "head", split_axis=0, concat_axis=1, tiled=True
        ),
        lax.all_to_all(
            key_gradient.astype(jnp.bfloat16), "head", split_axis=0, concat_axis=1, tiled=True
        ),
        lax.all_to_all(
            value_gradient.astype(jnp.bfloat16), "head", split_axis=0, concat_axis=1, tiled=True
        ),
    )
    return (query_out, key_out, value_out)


def lane_of(shape):
    return lax.broadcasted_iota(jnp.int32, shape, len(shape) - 1)


def pair_sums(kvs, marks, first, rows, allowed, left_ref, right_ref, both_ref, prob_ref, score_ref):
    tokens = kvs[0].shape[0]
    group = right_ref.shape[0]
    key_row = lax.broadcasted_iota(jnp.int32, (tokens, LANES), 0)
    lane = lane_of((tokens, LANES))
    for i, (kv, mark_from) in enumerate(zip(kvs, marks)):
        down = slice(i * tokens, (i + 1) * tokens)
        mark = mark_from + key_row // rows
        ones = jnp.where((lane < first) | (lane == mark), -1.0, 0.0)
        left_ref[down, 0:LANES] = kv
        left_ref[down, LANES:] = ones.astype(BF16)
    for e in range(group):
        both = lax.dot_general(
            left_ref[...],
            right_ref[e],
            (((1,), (1,)), ((), ())),
            preferred_element_type=F32,
        )
        across = slice(e * tokens, (e + 1) * tokens)
        for i in range(len(kvs)):
            down = slice(i * tokens, (i + 1) * tokens)
            prob = jnp.exp(both[down, 0:tokens])
            if i == 0 and allowed is not None:
                prob = jnp.where(allowed, prob, 0.0)
            score = prob * both[down, tokens:]
            prob_ref[down, across] = prob.astype(BF16)
            score_ref[down, across] = score.astype(BF16)
    pairs = both_ref[...].reshape(group * tokens, LANES)
    value_side = jnp.dot(prob_ref[...], pairs, preferred_element_type=F32)
    key_side = jnp.dot(score_ref[...], pairs, preferred_element_type=F32)
    low = lane_of(value_side.shape) < HEAD_WIDTH
    return jnp.where(low, key_side, value_side)


def pack_kernel(*refs):
    sources, (out_ref, same_ref, cross_ref) = refs[:7], refs[7:10]
    near, key_ref, sems = refs[10:17], refs[17], refs[18]
    pos_ref, q_ref, g_ref, k_ref, v_ref, n_ref, d_ref = near
    copies = [
        pltpu.make_async_copy(source, target, sems.at[i])
        for i, (source, target) in enumerate(zip(sources, near))
    ]
    for i in (5, 6, 0, 3, 4, 1, 2):
        copies[i].start()
    rows = q_ref.shape[0]
    tall = pos_ref.shape[1]
    planes = tall // rows
    chips = same_ref.shape[0]
    group = q_ref.shape[1] // k_ref.shape[1]
    block = lax.axis_index("ctx")
    odd_core = (block & 1) == 1
    lane = lane_of((rows, LANES))
    low = lane < HEAD_WIDTH
    scale = HEAD_WIDTH ** (-0.5)

    copies[5].wait()
    copies[6].wait()
    copies[0].wait()
    lead = jnp.floor(pos_ref[0:1, 0:1].astype(F32) / (tall // 2))
    eight = NOTE_ROWS
    sub = lax.broadcasted_iota(jnp.int32, (eight, LANES), 0)
    quarter = lane_of((eight, LANES)) // rows
    turns = []
    for s in range(PIECES):
        for t, ref in enumerate((n_ref, d_ref)):
            rest = ref[...]
            for _ in range(s):
                rest = rest - rest.astype(BF16).astype(F32)
            piece = rest.astype(BF16).astype(F32)
            turns.append([pltpu.roll(piece, d * rows, 1) if d else piece for d in range(planes)])
    for parity in range(2):
        for h in range(planes):
            note = jnp.where(sub == len(turns), lead, 0.0)
            for r, turn in enumerate(turns):
                for e in range(group):
                    head = group * parity + e
                    line = turn[(e - h) % planes][head : head + 1, :]
                    note = jnp.where((sub == r) & (quarter == e), line, note)
            note = note.astype(BF16)
            for c in range(parity, 2 * chips, 2):
                key_ref[c * planes + h, rows : rows + eight, :] = note

    copies[3].wait()
    copies[4].wait()
    for chip in range(chips):
        cols = slice(chip * LANES, (chip + 1) * LANES)
        k = k_ref[:, cols].astype(F32)
        v = v_ref[:, cols].astype(F32)
        even = jnp.where(low, k, pltpu.roll(v, HEAD_WIDTH, 1)).astype(BF16)
        odd = jnp.where(low, pltpu.roll(k, HEAD_WIDTH, 1), v).astype(BF16)
        for h in range(planes):
            key_ref[2 * chip * planes + h, 0:rows, :] = even
            key_ref[(2 * chip + 1) * planes + h, 0:rows, :] = odd

    out = pltpu.make_async_copy(key_ref, out_ref, sems.at[7])
    out.start()

    def query_tiles(m):
        cols = slice(m * LANES, (m + 1) * LANES)
        q = q_ref[:, cols].astype(F32) * scale
        g = g_ref[:, cols].astype(F32)
        even = jnp.where(low, q, pltpu.roll(g, HEAD_WIDTH, 1))
        odd = jnp.where(low, pltpu.roll(q, HEAD_WIDTH, 1), g)
        return even, odd

    copies[1].wait()
    copies[2].wait()
    pairs = group // 2
    for chip in range(chips):
        to = (block >> 1) ^ chip
        for e in range(pairs):
            here = query_tiles(2 * chip * pairs + e)
            there = query_tiles((2 * chip + 1) * pairs + e)
            for side in range(2):
                first, second = here[side], there[side]
                at = (2 * e + side) * rows
                same = jnp.where(odd_core, second, first).astype(BF16)
                cross = jnp.where(odd_core, first, second).astype(BF16)
                same_ref[to, at : at + rows, :] = same
                cross_ref[to, at : at + rows, :] = cross
    out.wait()


def join_kernel(same_ref, cross_ref, *out_refs):
    packet = same_ref.shape[1]
    for m, ref in enumerate(out_refs):
        ref[0:packet, :] = same_ref[CHIP_ORDER[m]]
        ref[packet : 2 * packet, :] = cross_ref[CHIP_ORDER[m]]


def prepare_kernel(same_ref, cross_ref, *refs):
    far_refs, both_ref = refs[:-1], refs[-1]
    group, tokens, _ = both_ref.shape
    packet = same_ref.shape[1]
    rows = packet // group
    block = lax.axis_index("ctx")
    slots = {0: same_ref.at[0], 1: cross_ref.at[0]}
    for m, ref in enumerate(far_refs):
        slots[2 * CHIP_ORDER[m]] = ref.at[0:packet]
        slots[2 * CHIP_ORDER[m] + 1] = ref.at[packet : 2 * packet]
    for i, slot in slots.items():
        at = pl.multiple_of((block ^ i) * rows, rows)
        for e in range(group):
            both_ref[e, pl.ds(at, rows), :] = slot[e * rows : (e + 1) * rows, :]


def plane_keys(key_ref, which, blocks, rows):
    planes = key_ref.shape[0] // blocks
    return jnp.concatenate([key_ref[b * planes + which, 0:rows, :] for b in range(blocks)], 0)


def attend_kernel(
    both_ref, key_ref, out_ref, same_ref, cross_ref,
    scores_ref, right_ref, wide_ref, left_ref, prob_ref, part_ref, all_ref, sems,
):
    group, tokens, _ = both_ref.shape
    blocks, planes, rows, _ = out_ref.shape
    eight = NOTE_ROWS
    count = 2 * PIECES
    plane = lax.axis_index("head")
    holder = lax.axis_index("ctx") // (blocks // planes)
    first = LANES // 2
    lane = lane_of((rows, LANES))
    lane_row = lane_of((1, LANES))
    quarter = lane_of((eight, LANES)) // rows

    lead = jnp.zeros((1, LANES), F32)
    notes = []
    for b in range(blocks):
        note = key_ref[b * planes + holder, rows : rows + eight, :].astype(F32)
        lead = jnp.where(lane_row % blocks == b, note[count : count + 1], lead)
        notes.append(note)
    wide_ref[...] = jnp.zeros(wide_ref.shape, F32)
    per_tile = LANES // rows
    for e in range(group):
        for b in range(blocks):
            spot = b % per_tile
            turn = ((spot - e) * rows) % LANES
            moved = pltpu.roll(notes[b], turn, 1) if turn else notes[b]
            down = slice((b // per_tile) * LANES + e * eight, (b // per_tile) * LANES + (e + 1) * eight)
            wide_ref[down, :] = jnp.where(quarter == spot, moved, wide_ref[down, :])
    low = lane_of((tokens, LANES)) < HEAD_WIDTH
    nothing = jnp.zeros((tokens, LANES), BF16)
    for e in range(group):
        right_ref[e, 0:tokens, 0:LANES] = jnp.where(low, both_ref[e], nothing)
        right_ref[e, tokens : 2 * tokens, 0:LANES] = jnp.where(low, nothing, both_ref[e])
    columns = [
        wide_ref[m * LANES : (m + 1) * LANES, :].T for m in range(tokens // LANES)
    ]

    key_plane = (lane_row - first) // blocks
    per_half = planes // 2

    def place(lead_of, which):
        front = per_half * lead_of + which
        back = per_half * (2 * blocks - 1 - lead_of) + (which - per_half)
        return jnp.where(which < per_half, front, back)

    key_place = place(lead, key_plane.astype(F32))
    in_mask = (lane_row >= first) & (lane_row < first + planes * blocks)
    for b in range(blocks):
        lead_b = jnp.sum(jnp.where(lane_row == first + b, lead, 0.0), axis=1, keepdims=True)
        query_place = place(lead_b, plane.astype(F32))
        hidden = jnp.where(in_mask & (key_place > query_place), MASKED, 0.0)
        at = (b % per_tile) * rows
        column = columns[b // per_tile][at : at + rows]
        for e in range(group):
            mine = (lane >= e * eight) & (lane < e * eight + count)
            norm = jnp.where(mine & (lane % 2 == 0), column, hidden)
            delta = jnp.where(mine & (lane % 2 == 1), column, 0.0)
            right_ref[e, b * rows : (b + 1) * rows, LANES:] = norm.astype(BF16)
            down = slice(tokens + b * rows, tokens + (b + 1) * rows)
            right_ref[e, down, LANES:] = delta.astype(BF16)

    square_key = lax.broadcasted_iota(jnp.int32, (tokens, tokens), 0)
    square_query = lane_of((tokens, tokens))
    allowed = (square_key <= square_query) | (square_key // rows != square_query // rows)
    copies = []
    for j in range(0, planes, TOGETHER):
        group_of = [plane ^ (j + i) for i in range(TOGETHER)]
        kv_sum = pair_sums(
            [plane_keys(key_ref, which, blocks, rows) for which in group_of],
            [first + which * blocks for which in group_of],
            first, rows, None if j else allowed,
            left_ref, right_ref, both_ref, prob_ref,
            scores_ref.at[j * tokens : (j + TOGETHER) * tokens],
        ).astype(BF16)
        for i, which in enumerate(group_of):
            part = kv_sum[i * tokens : (i + 1) * tokens]
            part_ref[j + i] = part.reshape(blocks, rows, LANES)
            copy = pltpu.make_async_copy(part_ref.at[j + i], out_ref.at[:, which], sems.at[j + i])
            copy.start()
            copies.append(copy)
    query_sum = jnp.zeros((HEAD_WIDTH, group * tokens), F32)
    for j in range(planes):
        keys = plane_keys(key_ref, plane ^ j, blocks, rows)
        turned = keys.astype(F32).T[0:HEAD_WIDTH].astype(BF16)
        here = scores_ref[j * tokens : (j + 1) * tokens, :]
        query_sum = query_sum + jnp.dot(turned, here, preferred_element_type=F32)
    scale = HEAD_WIDTH ** (-0.5)
    for m in range(group // 2):
        pair = jnp.concatenate(
            [
                query_sum[:, 2 * m * tokens : (2 * m + 1) * tokens],
                query_sum[:, (2 * m + 1) * tokens : (2 * m + 2) * tokens],
            ],
            0,
        )
        done = (pair.T * scale).astype(BF16)
        all_ref[:, m * rows : (m + 1) * rows, :] = done.reshape(blocks, rows, LANES)
    block = lax.axis_index("ctx")
    for m in range(blocks // 2):
        same_ref[m] = all_ref[block ^ (2 * m)]
        cross_ref[m] = all_ref[block ^ (2 * m + 1)]
    for copy in copies:
        copy.wait()


def unpack_kernel(part_ref, same_ref, cross_ref, *refs):
    chips = same_ref.shape[0]
    far_refs, (q_ref, k_ref, v_ref, all_ref) = refs[: chips - 1], refs[chips - 1 :]
    rows = q_ref.shape[0]
    tall = same_ref.shape[1]
    tiles = tall // rows
    planes = part_ref.shape[0] // (2 * chips)
    block = lax.axis_index("ctx")
    all_ref[block] = same_ref[0]
    all_ref[block ^ 1] = cross_ref[0]
    for m, ref in enumerate(far_refs):
        chip = 2 * CHIP_ORDER[m]
        all_ref[block ^ chip] = ref[0:tall, :]
        all_ref[block ^ (chip + 1)] = ref[tall : 2 * tall, :]
    for c in range(2 * chips):
        for m in range(tiles):
            at = (c * tiles + m) * LANES
            q_ref[:, at : at + LANES] = all_ref[c, m * rows : (m + 1) * rows, :]

    def added(c):
        total = part_ref[c * planes].astype(F32)
        for h in range(1, planes):
            total = total + part_ref[c * planes + h].astype(F32)
        return total

    low = lane_of((rows, LANES)) < HEAD_WIDTH
    for m in range(chips):
        even, odd = added(2 * m), added(2 * m + 1)
        cols = slice(m * LANES, (m + 1) * LANES)
        k_ref[:, cols] = jnp.where(low, even, pltpu.roll(odd, HEAD_WIDTH, 1)).astype(BF16)
        v_ref[:, cols] = jnp.where(low, pltpu.roll(even, HEAD_WIDTH, 1), odd).astype(BF16)


def whole(shape):
    return pl.BlockSpec(shape, lambda: (0,) * len(shape))


ROOMY = pltpu.CompilerParams(vmem_limit_bytes=24 << 20)
KEPT = pl.BlockSpec(memory_space=pltpu.VMEM)


def kept(*arrays):
    return [pltpu.with_memory_space_constraint(a, pltpu.VMEM) for a in arrays]


def by_heads(
    query_input,
    key_input,
    value_input,
    output_gradient,
    log_softmax_norm,
    output_delta_rows,
    positions,
):
    blocks = lax.axis_size("ctx")
    planes = lax.axis_size("head")
    rows = query_input.shape[0]
    tokens = blocks * rows
    group = query_input.shape[1] // key_input.shape[1]
    packet = group * rows
    chips = blocks // 2
    devices = blocks * planes
    wide = group * tokens
    arguments = (
        positions.reshape(1, -1),
        query_input,
        output_gradient,
        key_input,
        value_input,
        log_softmax_norm.T,
        output_delta_rows.T,
    )
    half = pltpu.VMEM((chips, packet, LANES), BF16)
    keys, same, cross = pl.pallas_call(
        pack_kernel,
        name="pack",
        compiler_params=ROOMY,
        out_shape=[jax.ShapeDtypeStruct((devices, rows + NOTE_ROWS, LANES), BF16), half, half],
        in_specs=[pl.BlockSpec(memory_space=pl.ANY)] * len(arguments),
        out_specs=[pl.BlockSpec(memory_space=pl.ANY), KEPT, KEPT],
        scratch_shapes=[
            pltpu.VMEM(a.shape, a.dtype) for a in arguments
        ]
        + [
            pltpu.VMEM((devices, rows + NOTE_ROWS, LANES), BF16),
            pltpu.SemaphoreType.DMA((len(arguments) + 1,)),
        ],
    )(*[pltpu.with_memory_space_constraint(a, pltpu.HBM) for a in arguments])

    def trade(array, by):
        return lax.ppermute(array, "ctx", [(i, i ^ by) for i in range(blocks)])

    def to_all(array):
        return lax.all_to_all(array, ("ctx", "head"), split_axis=0, concat_axis=0, tiled=True)

    keys = to_all(keys)

    def exchange(same, cross):
        tall = same.shape[1]
        cross = trade(cross, 1)
        joined = pl.pallas_call(
            join_kernel,
            name="join",
            compiler_params=ROOMY,
            out_shape=[pltpu.VMEM((2 * tall, LANES), BF16)] * (chips - 1),
            in_specs=[KEPT] * 2,
            out_specs=[KEPT] * (chips - 1),
        )(*kept(same, cross))
        joined = [trade(array, 2 * CHIP_ORDER[m]) for m, array in enumerate(joined)]
        return kept(same, cross, *joined)

    received = exchange(same, cross)
    both = pl.pallas_call(
        prepare_kernel,
        name="prepare",
        compiler_params=ROOMY,
        out_shape=pltpu.VMEM((group, tokens, LANES), BF16),
        in_specs=[KEPT] * (chips + 1),
        out_specs=KEPT,
    )(*received)
    (keys,) = kept(keys)
    tall = group // 2 * rows
    half = pltpu.VMEM((chips, tall, LANES), BF16)
    parts, same, cross = pl.pallas_call(
        attend_kernel,
        name="attend",
        compiler_params=ROOMY,
        out_shape=[jax.ShapeDtypeStruct((blocks, planes, rows, LANES), BF16), half, half],
        in_specs=[KEPT] * 2,
        out_specs=[pl.BlockSpec(memory_space=pl.ANY), KEPT, KEPT],
        scratch_shapes=[
            pltpu.VMEM((planes * tokens, wide), BF16),
            pltpu.VMEM((group, 2 * tokens, 2 * LANES), BF16),
            pltpu.VMEM((tokens // LANES * LANES, LANES), F32),
            pltpu.VMEM((TOGETHER * tokens, 2 * LANES), BF16),
            pltpu.VMEM((TOGETHER * tokens, wide), BF16),
            pltpu.VMEM((planes, blocks, rows, LANES), BF16),
            pltpu.VMEM((blocks, tall, LANES), BF16),
            pltpu.SemaphoreType.DMA((planes,)),
        ],
    )(*kept(both), keys)
    parts = to_all(parts.reshape(devices, rows, LANES))
    received = exchange(same, cross)
    shapes = [query_input.shape, key_input.shape, value_input.shape]
    return tuple(
        pl.pallas_call(
            unpack_kernel,
            name="unpack",
            compiler_params=ROOMY,
            out_shape=[jax.ShapeDtypeStruct(s, BF16) for s in shapes],
            in_specs=[KEPT] * (chips + 2),
            out_specs=[whole(s) for s in shapes],
            scratch_shapes=[pltpu.VMEM((blocks, tall, LANES), BF16)],
        )(*kept(parts), *received)
    )


def solution(mesh):
    def on_each(*args):
        query_input, key_input = args[0], args[1]
        kv_heads = key_input.shape[1] // HEAD_WIDTH
        group = query_input.shape[1] // key_input.shape[1]
        blocks, planes = mesh.shape["ctx"], mesh.shape["head"]
        by_head = (
            blocks == kv_heads
            and group == 4
            and planes == 4
            and kv_heads == 8
            and query_input.shape[0] % 16 == 0
        )
        return (by_heads if by_head else on_device)(*args)

    return jax.shard_map(
        on_each,
        mesh=mesh,
        in_specs=(
            P(("ctx", "head"), None),
            P(("ctx", "head"), None),
            P(("ctx", "head"), None),
            P(("ctx", "head"), None),
            P("ctx", "head"),
            P("ctx", "head"),
            P("ctx"),
        ),
        out_specs=(P(("ctx", "head"), None), P(("ctx", "head"), None), P(("ctx", "head"), None)),
        check_vma=False,
    )
```
